128 devices in a mesh: dp: 8 (over z, core), tensor: 16 (over x, y).
Axes of the slice: x: 4, y: 4, z: 4, core: 2. Of those that a mesh axis runs over, the one named last changes fastest.
Arguments:
- residual_in: bfloat16 [1024, 4096], P('dp'), may hold values from -3 to 3
- query: bfloat16 [1024, 8192], P('dp', 'tensor'), may hold values from -130 to 130
- fresh_key: bfloat16 [1024, 4, 128], P('dp'), may hold values from -5 to 5
- fresh_value: bfloat16 [1024, 4, 128], P('dp'), may hold values from -10 to 10
- key_cache: bfloat16 [1024, 16, 128, 128], P('dp', 'tensor'), may hold values from -5 to 5, as said below
- value_cache: bfloat16 [1024, 16, 128, 128], P('dp', 'tensor'), may hold values from -10 to 10, as said below
- lengths: int32 [1024], P('dp'), may hold values from 2 to 128
- out_weight: bfloat16 [8192, 4096], P('tensor'), may hold values from -0.0625 to 0.0625
- norm_gain: float32 [4096], replicated, may hold values from 0.1 to 1.9
- expert_ids: int32 [1024, 8], P('dp'), may hold values from 0 to 127, all different within a row; in each aligned block of 128 rows (0 to 127, 128 to 255, ...) at most 16 rows name the same one
- gate_scores: float32 [1024, 8], P('dp'), may hold values from 0.05 to 1
- w_gate: bfloat16 [128, 4096, 768], P(('dp', 'tensor')), may hold values from -0.09375 to 0.09375
- w_up: bfloat16 [128, 4096, 768], P(('dp', 'tensor')), may hold values from -0.09375 to 0.09375
- w_down: bfloat16 [128, 768, 4096], P(('dp', 'tensor')), may hold values from -0.21875 to 0.21875
Outputs:
- layer_out: bfloat16 [1024, 4096], P(('dp', 'tensor'))
The draws below stay inside these ranges and needn't reach their ends.
Inputs may be any that keep to these rules, and one draw needn't show every extreme that they name: `expert_ids`: each row names 8 different experts; among the 128 rows of one data replica (aligned blocks) no expert is named by more than 16 rows, a bound that some block reaches. `key_cache`: the copies of one key head are equal. `value_cache`: the copies of one value head are equal.
All inputs are finite; a program needn't handle non-finite values.
Results may differ from the reference program's by a relative error of at most 0.023.
Values may be sent and summed in bfloat16 or wider, within the bound.
No kernel may reach another device: no remote copies, remote signals or barrier semaphores. Data moves between devices by JAX's collectives and lax.ppermute only.
A program may use at most 128 MiB of HBM per device.

```python
import math
import jax
import jax.numpy as jnp
import numpy as np
from jax import lax

D = 4096
QUERY_HEADS = 64
KEY_HEADS = 4
HEAD_SIZE = 128
FF_WIN = 768
TOPK = 8
ROWS_DEV = 128
CACHED_POSITIONS = 128
DECODE_ROWS = 1024
EXPERTS = 128
CAP = 16
N_DP = 8
N_TENSOR = 16


def cache_base(key):
    return jnp.clip(jax.random.normal(jax.random.fold_in(key, 11), (DECODE_ROWS, KEY_HEADS, CACHED_POSITIONS, HEAD_SIZE), jnp.float32), -5.0, 5.0)


def draw_key_cache(key, part):
    base_offset = cache_base(key)
    return jnp.repeat(base_offset, N_TENSOR // KEY_HEADS, axis=1).astype(jnp.bfloat16)


def draw_value_cache(key, part):
    base_offset = jnp.clip(2.0 * jax.random.normal(jax.random.fold_in(key, 31), (DECODE_ROWS, KEY_HEADS, CACHED_POSITIONS, HEAD_SIZE), jnp.float32), -10.0, 10.0)
    return jnp.repeat(base_offset, N_TENSOR // KEY_HEADS, axis=1).astype(jnp.bfloat16)


def draw_query(key, part):
    entries = jnp.clip(jax.random.normal(jax.random.fold_in(key, 12), (DECODE_ROWS, QUERY_HEADS, HEAD_SIZE), jnp.float32), -5.0, 5.0)
    return entries.reshape(DECODE_ROWS, QUERY_HEADS * HEAD_SIZE).astype(jnp.bfloat16)


def draw_lengths(key, part):
    drawn = jax.random.randint(jax.random.fold_in(key, 21), (DECODE_ROWS,), 2, CACHED_POSITIONS + 1, dtype=jnp.int32)
    return drawn.at[0].set(CACHED_POSITIONS)


def shard_levels(rng, extent, pieces, smallest, largest):
    gain, own = 1.0, jax.random.fold_in(rng, 6)
    for position, parts in pieces:
        heights = jnp.exp(jax.random.uniform(jax.random.fold_in(own, position), (parts,), jnp.float32, smallest / len(pieces), largest / len(pieces)))
        gain = gain * jnp.repeat(heights, extent[position] // parts).reshape([-1 if axis == position else 1 for axis in range(len(extent))])
    return gain


def routed_block(own_key, own, number, rows, amount, top, bound, skew):
    order = jax.random.permutation(own_key, amount)
    heavy_load, common = shares(amount, rows * top, bound, skew, True), shares(amount, rows * top, bound, skew, False)
    places = jnp.arange(amount)

    def named(sizes, turn):
        used = int((sizes > 0).sum())
        fixed = max(1, used // 4)
        shifted = fixed + (places - fixed + turn * (used - fixed)) % max(1, amount - fixed)
        return jnp.zeros((amount,), jnp.int32).at[order[jnp.where(places < fixed, places, shifted)]].set(jnp.asarray(sizes, jnp.int32))

    sizes = jnp.where(number % 4 == 0, named(heavy_load, number // 4), named(common, number - number // 4 - 1))
    mixed = jax.random.permutation(jax.random.fold_in(own, 3), amount)
    giver, taker = mixed[0:amount // 2 * 2:2], mixed[1:amount // 2 * 2:2]
    margin = jnp.minimum(sizes[giver] - 1, bound - sizes[taker]) // 2
    margin = jnp.where((giver == order[0]) | (taker == order[0]) | (sizes[taker] == 0), 0, jnp.maximum(margin, 0))
    shifted = jax.random.randint(jax.random.fold_in(own, 4), (amount // 2,), 0, 1 << 20) % (margin + 1)
    sizes = sizes.at[giver].add(-shifted).at[taker].add(shifted)
    members = jnp.searchsorted(jnp.cumsum(sizes), jnp.arange(rows * top), side="right").astype(jnp.int32)
    table = members.reshape(top, rows).T
    table = table[jax.random.permutation(jax.random.fold_in(own, 1), rows)]
    turn = jax.random.randint(jax.random.fold_in(own, 2), (rows, 1), 0, top)
    return jnp.take_along_axis(table, (jnp.arange(top)[None, :] + turn) % top, axis=1)


def shares(amount, total, most, slope, full):
    portions = [(1 << 20) // math.isqrt(rank ** slope) + 1 for rank in range(1, amount + 1)]
    largest = most if full else min(most, max(-(-total // amount), total * portions[0] // sum(portions)))
    least = 1 if total - largest >= amount - 1 else 0
    holding, surplus = [largest] + [least] * (amount - 1), total - largest - least * (amount - 1)
    while surplus > 0:
        movable = [i for i in range(1, amount) if holding[i] < largest] or [i for i in range(1, amount) if holding[i] < most]
        mass, budget = sum([portions[i] for i in movable]), surplus
        for i in movable:
            addition = min(most - holding[i], max(1, budget * portions[i] // mass), surplus)
            holding[i] = holding[i] + addition
            surplus = surplus - addition
    return np.array(holding)


def normal_values(own_key, shape, scale, limit, pieces=(), kind=jnp.bfloat16):
    array = jax.random.normal(own_key, shape, jnp.float32) * scale
    if len(pieces) > 0:
        array = shard_levels(own_key, shape, pieces, -0.22, 0.18) * array
    return jnp.clip(array, min=-limit, max=limit).astype(kind)


def setup_inputs(seed: int = 0) -> dict:
    key_list = jax.random.split(jax.random.key(seed), 15)
    residual_in = normal_values(key_list[0], (DECODE_ROWS, D), 0.5, 3.0, ((0, 8),))
    query = draw_query(jax.random.fold_in(key_list[14], 71), 0)
    fresh_key = normal_values(key_list[2], (DECODE_ROWS, KEY_HEADS, HEAD_SIZE), 1.0, 5.0, ((0, 8),))
    fresh_value = normal_values(key_list[3], (DECODE_ROWS, KEY_HEADS, HEAD_SIZE), 2.0, 10.0, ((0, 8),))
    key_cache = draw_key_cache(jax.random.fold_in(key_list[14], 71), 0)
    value_cache = draw_value_cache(jax.random.fold_in(key_list[14], 71), 0)
    lengths = draw_lengths(jax.random.fold_in(key_list[14], 71), 0)
    out_weight = normal_values(key_list[7], (QUERY_HEADS * HEAD_SIZE, D), (QUERY_HEADS * HEAD_SIZE) ** -0.5, 0.0625, ((0, 16),))
    norm_gain = jnp.clip(1.0 + 0.18 * jax.random.normal(key_list[8], (D,), jnp.float32), 0.1, 1.9)
    expert_ids_keys = jax.random.split(jax.random.fold_in(key_list[9], 1), DECODE_ROWS // ROWS_DEV)
    expert_ids_turns = jax.random.permutation(jax.random.fold_in(key_list[9], 3), DECODE_ROWS // ROWS_DEV)
    expert_ids = jax.vmap(lambda own, number: routed_block(jax.random.fold_in(key_list[9], 2), own, number, ROWS_DEV, EXPERTS, TOPK, CAP, 2))(expert_ids_keys, expert_ids_turns).reshape((DECODE_ROWS, TOPK))
    gate_scores = jnp.clip(jnp.exp(math.log(1.0) - 2.9957323 * jax.random.uniform(key_list[10], (DECODE_ROWS, TOPK), jnp.float32) ** shard_levels(key_list[10], (DECODE_ROWS, TOPK), ((0, 8),), -0.2, 0.2)), 0.05, 1.0)
    w_gate = normal_values(key_list[11], (EXPERTS, D, FF_WIN), D ** -0.5, 0.09375, ((0, 128),))
    w_up = normal_values(key_list[12], (EXPERTS, D, FF_WIN), D ** -0.5, 0.09375, ((0, 128),))
    w_down = normal_values(key_list[13], (EXPERTS, FF_WIN, D), FF_WIN ** -0.5, 0.21875, ((0, 128),))
    return {"residual_in": residual_in, "query": query, "fresh_key": fresh_key, "fresh_value": fresh_value, "key_cache": key_cache, "value_cache": value_cache, "lengths": lengths, "out_weight": out_weight, "norm_gain": norm_gain, "expert_ids": expert_ids, "gate_scores": gate_scores, "w_gate": w_gate, "w_up": w_up, "w_down": w_down}


def rms_normalize(hidden, norm_gain):
    widened = hidden.astype(jnp.float32)
    spread = lax.optimization_barrier(jnp.mean(widened * widened, axis=-1, keepdims=True))
    return (widened * lax.rsqrt(spread + 1e-06) * norm_gain.astype(jnp.float32)).astype(jnp.bfloat16)

def reference(residual_in, query, fresh_key, fresh_value, key_cache, value_cache, lengths, out_weight, norm_gain, expert_ids, gate_scores, w_gate, w_up, w_down):
    head_copies = N_TENSOR // KEY_HEADS
    query_group = QUERY_HEADS // KEY_HEADS
    score_scale = HEAD_SIZE ** (-0.5)
    query_rows = query.astype(jnp.float32).reshape(DECODE_ROWS, KEY_HEADS, query_group, HEAD_SIZE)
    cached_keys = key_cache[:, ::head_copies].astype(jnp.float32)
    cached_values = value_cache[:, ::head_copies].astype(jnp.float32)
    scores = jnp.einsum('rkgd,rkpd->rkgp', query_rows, cached_keys) * score_scale
    own_score = jnp.einsum('rkgd,rkd->rkg', query_rows, fresh_key.astype(jnp.float32)) * score_scale
    in_cache = jnp.arange(CACHED_POSITIONS, dtype=jnp.int32)[None, :] < lengths[:, None]
    scores = jnp.where(in_cache[:, None, None, :], scores, -1e+30)
    row_max = jnp.maximum(lax.optimization_barrier(jnp.max(scores, axis=-1)), own_score)
    cache_terms = jnp.exp(scores - row_max[..., None])
    own_term = jnp.exp(own_score - row_max)
    denom = lax.optimization_barrier(jnp.sum(cache_terms, axis=-1)) + own_term
    probs = (cache_terms / denom[..., None]).astype(jnp.bfloat16)
    own_prob = (own_term / denom).astype(jnp.bfloat16)
    attended = jnp.einsum('rkgp,rkpd->rkgd', probs.astype(jnp.float32), cached_values)
    attended = attended + own_prob.astype(jnp.float32)[..., None] * fresh_value.astype(jnp.float32)[:, :, None, :]
    heads_out = attended.astype(jnp.bfloat16).reshape(DECODE_ROWS, QUERY_HEADS * HEAD_SIZE)
    proj = jnp.dot(heads_out, out_weight, preferred_element_type=jnp.float32)
    hidden = (residual_in.astype(jnp.float32) + proj).astype(jnp.bfloat16)
    normed = rms_normalize(hidden, norm_gain)
    weights = gate_scores / lax.optimization_barrier(jnp.sum(gate_scores, axis=1, keepdims=True))
    slots = N_DP * CAP

    def one_expert(partial_value, expert):
        gate_mat = lax.dynamic_index_in_dim(w_gate, expert, 0, keepdims=False)
        up_mat = lax.dynamic_index_in_dim(w_up, expert, 0, keepdims=False)
        down_mat = lax.dynamic_index_in_dim(w_down, expert, 0, keepdims=False)
        chosen = expert_ids == expert
        routed = jnp.any(chosen, axis=1)
        row_weight = lax.optimization_barrier(jnp.sum(jnp.where(chosen, weights, 0.0), axis=1))
        picked_rows = jnp.argsort(jnp.where(routed, 0, 1).astype(jnp.int32), stable=True)[:slots].astype(jnp.int32)
        inputs_rows = normed[picked_rows]
        gate_part = jnp.dot(inputs_rows, gate_mat, preferred_element_type=jnp.float32)
        up_part = jnp.dot(inputs_rows, up_mat, preferred_element_type=jnp.float32)
        act = (jax.nn.silu(gate_part) * up_part).astype(jnp.bfloat16)
        expert_out = jnp.dot(act, down_mat, preferred_element_type=jnp.float32).astype(jnp.bfloat16)
        partial_value = partial_value.at[picked_rows].add(row_weight[picked_rows][:, None] * expert_out.astype(jnp.float32))
        return (partial_value, None)

    def one_column(mixture, column_index):
        experts_here = jnp.arange(N_DP, dtype=jnp.int32) * N_TENSOR + column_index
        start_part = jnp.zeros((DECODE_ROWS, D), jnp.float32)
        partial_value, unused = lax.scan(one_expert, start_part, experts_here)
        return (mixture + partial_value.astype(jnp.bfloat16).astype(jnp.float32), None)
    start_mix = jnp.zeros((DECODE_ROWS, D), jnp.float32)
    mixture, unused = lax.scan(one_column, start_mix, jnp.arange(N_TENSOR, dtype=jnp.int32))
    return (hidden.astype(jnp.float32) + mixture).astype(jnp.bfloat16)
```

```python
import jax
import jax.numpy as jnp
from jax import lax
from jax.sharding import PartitionSpec as P


def attend(query, fresh_key, fresh_value, key_cache, value_cache, lengths, column, tensor_width):
    row_count = query.shape[0]
    head_size = key_cache.shape[3]
    kv_head = column // (tensor_width // fresh_key.shape[1])
    head_count = query.shape[1] // head_size
    score_scale = head_size ** (-0.5)
    query_rows = query.reshape(row_count, head_count, head_size)
    cached_keys = key_cache[:, 0]
    cached_values = value_cache[:, 0]
    own_key = lax.dynamic_index_in_dim(fresh_key, kv_head, 1, keepdims=False)
    own_value = lax.dynamic_index_in_dim(fresh_value, kv_head, 1, keepdims=False)
    scores = (
        jnp.einsum("rhd,rpd->rhp", query_rows, cached_keys, preferred_element_type=jnp.float32)
        * score_scale
    )
    own_score = (
        jnp.einsum("rhd,rd->rh", query_rows, own_key, preferred_element_type=jnp.float32)
        * score_scale
    )
    in_cache = (
        lax.broadcasted_iota(jnp.int32, (row_count, cached_keys.shape[1]), 1) < lengths[:, None]
    )
    scores = jnp.where(in_cache[:, None, :], scores, -1e30)
    row_max = jnp.maximum(jnp.max(scores, axis=-1), own_score)
    cache_terms = jnp.exp(scores - row_max[..., None])
    own_term = jnp.exp(own_score - row_max)
    denom = jnp.sum(cache_terms, axis=-1) + own_term
    probs = (cache_terms / denom[..., None]).astype(jnp.bfloat16)
    own_prob = (own_term / denom).astype(jnp.bfloat16)
    attended = jnp.einsum("rhp,rpd->rhd", probs, cached_values, preferred_element_type=jnp.float32)
    attended = (
        attended
        + own_prob.astype(jnp.float32)[..., None] * own_value.astype(jnp.float32)[:, None, :]
    )
    return attended.astype(jnp.bfloat16).reshape(row_count, head_count * head_size)


def route(expert_ids, gate_scores, experts_all):
    row_count = expert_ids.shape[0]
    expert_axis = lax.broadcasted_iota(jnp.int32, (1, 1, experts_all), 2)
    matches = expert_ids[:, :, None] == expert_axis
    weights = gate_scores / jnp.sum(gate_scores, axis=1, keepdims=True)
    row_weight = jnp.sum(jnp.where(matches, weights[:, :, None], 0.0), axis=1).T
    routed = jnp.any(matches, axis=1).astype(jnp.bfloat16).T
    before = (
        lax.broadcasted_iota(jnp.int32, (row_count, row_count), 0)
        < lax.broadcasted_iota(jnp.int32, (row_count, row_count), 1)
    ).astype(jnp.bfloat16)
    rank = jnp.dot(routed, before, preferred_element_type=jnp.float32)
    slot = jnp.where(routed > 0, rank, -1.0).astype(jnp.int32)
    return slot, row_weight


def shards(
    residual_in,
    query,
    fresh_key,
    fresh_value,
    key_cache,
    value_cache,
    lengths,
    out_weight,
    norm_gain,
    expert_ids,
    gate_scores,
    w_gate,
    w_up,
    w_down,
):
    both = ("dp", "tensor")
    row_count, width = residual_in.shape
    tensor_width = lax.axis_size("tensor")
    replica_count = lax.axis_size("dp")
    experts_all = replica_count * tensor_width
    column = lax.axis_index("tensor")
    chunk = width // tensor_width
    cap_slots = 2 * max(1, row_count * expert_ids.shape[1] // experts_all)

    heads_out = attend(
        query, fresh_key, fresh_value, key_cache, value_cache, lengths, column, tensor_width
    )
    partial = jnp.einsum(
        "rk,ktj->trj",
        heads_out,
        out_weight.reshape(-1, tensor_width, chunk),
        preferred_element_type=jnp.float32,
    ).astype(jnp.bfloat16)
    pieces = lax.all_to_all(partial, "tensor", split_axis=0, concat_axis=0, tiled=True)
    proj = jnp.sum(pieces.astype(jnp.float32), axis=0)
    residual = lax.dynamic_slice_in_dim(residual_in, column * chunk, chunk, 1)
    hidden = (residual.astype(jnp.float32) + proj).astype(jnp.bfloat16)

    slot, row_weight = route(expert_ids, gate_scores, experts_all)
    slot_axis = lax.broadcasted_iota(jnp.int32, (1, cap_slots, 1), 1)
    chosen = slot[:, None, :] == slot_axis
    outgoing = jnp.einsum(
        "esr,rj->esj", chosen.astype(jnp.bfloat16), hidden, preferred_element_type=jnp.float32
    ).astype(jnp.bfloat16)
    received = lax.all_to_all(outgoing, both, split_axis=0, concat_axis=0, tiled=True)

    rows = received.reshape(replica_count, tensor_width, cap_slots, chunk)
    rows = rows.transpose(0, 2, 1, 3).reshape(replica_count * cap_slots, width)
    widened = rows.astype(jnp.float32)
    spread = jnp.mean(widened * widened, axis=-1, keepdims=True)
    normed = (widened * lax.rsqrt(spread + 1e-06) * norm_gain).astype(jnp.bfloat16)
    gate_part = jnp.dot(normed, w_gate[0], preferred_element_type=jnp.float32)
    up_part = jnp.dot(normed, w_up[0], preferred_element_type=jnp.float32)
    act = (jax.nn.silu(gate_part) * up_part).astype(jnp.bfloat16)
    result = jnp.dot(act, w_down[0], preferred_element_type=jnp.float32).astype(jnp.bfloat16)
    result = result.reshape(replica_count, cap_slots, tensor_width, chunk).transpose(0, 2, 1, 3)
    answered = result.reshape(experts_all, cap_slots, chunk)
    returned = lax.all_to_all(answered, both, split_axis=0, concat_axis=0, tiled=True)

    spread_weight = jnp.where(chosen, row_weight[:, None, :], 0.0)
    coarse = spread_weight.astype(jnp.bfloat16)
    fine = (spread_weight - coarse.astype(jnp.float32)).astype(jnp.bfloat16)
    mixture = jnp.einsum(
        "esr,esj->rj", coarse, returned, preferred_element_type=jnp.float32
    ) + jnp.einsum("esr,esj->rj", fine, returned, preferred_element_type=jnp.float32)
    layer = (hidden.astype(jnp.float32) + mixture).astype(jnp.bfloat16)
    own = lax.all_to_all(
        layer.reshape(tensor_width, row_count // tensor_width, chunk),
        "tensor",
        split_axis=0,
        concat_axis=0,
        tiled=True,
    )
    return own.transpose(1, 0, 2).reshape(row_count // tensor_width, width)


def solution(mesh):
    placed = (
        P("dp", None),
        P("dp", "tensor"),
        P("dp", None, None),
        P("dp", None, None),
        P("dp", "tensor", None, None),
        P("dp", "tensor", None, None),
        P("dp"),
        P("tensor", None),
        P(),
        P("dp", None),
        P("dp", None),
        P(("dp", "tensor"), None, None),
        P(("dp", "tensor"), None, None),
        P(("dp", "tensor"), None, None),
    )
    return jax.shard_map(
        shards, mesh=mesh, in_specs=placed, out_specs=P(("dp", "tensor"), None), check_vma=False
    )
```

```python
import jax
import jax.numpy as jnp
from jax import lax
from jax.experimental import pallas as pl
from jax.experimental.pallas import tpu as pltpu
from jax.sharding import PartitionSpec as P


def attend(query, fresh_key, fresh_value, key_cache, value_cache, lengths, column, tensor_width):
    row_count = query.shape[0]
    head_size = key_cache.shape[3]
    kv_head = column // (tensor_width // fresh_key.shape[1])
    head_count = query.shape[1] // head_size
    score_scale = head_size ** (-0.5)
    query_rows = query.reshape(row_count, head_count, head_size)
    cached_keys = key_cache[:, 0]
    cached_values = value_cache[:, 0]
    own_key = lax.dynamic_index_in_dim(fresh_key, kv_head, 1, keepdims=False)
    own_value = lax.dynamic_index_in_dim(fresh_value, kv_head, 1, keepdims=False)
    scores = (
        jnp.einsum("rhd,rpd->rhp", query_rows, cached_keys, preferred_element_type=jnp.float32)
        * score_scale
    )
    own_score = (
        jnp.einsum("rhd,rd->rh", query_rows, own_key, preferred_element_type=jnp.float32)
        * score_scale
    )
    in_cache = (
        lax.broadcasted_iota(jnp.int32, (row_count, cached_keys.shape[1]), 1) < lengths[:, None]
    )
    scores = jnp.where(in_cache[:, None, :], scores, -1e30)
    row_max = jnp.maximum(jnp.max(scores, axis=-1), own_score)
    cache_terms = jnp.exp(scores - row_max[..., None])
    own_term = jnp.exp(own_score - row_max)
    denom = jnp.sum(cache_terms, axis=-1) + own_term
    probs = (cache_terms / denom[..., None]).astype(jnp.bfloat16)
    own_prob = (own_term / denom).astype(jnp.bfloat16)
    attended = jnp.einsum("rhp,rpd->rhd", probs, cached_values, preferred_element_type=jnp.float32)
    attended = (
        attended
        + own_prob.astype(jnp.float32)[..., None] * own_value.astype(jnp.float32)[:, None, :]
    )
    return attended.astype(jnp.bfloat16).reshape(row_count, head_count * head_size)


def route(expert_ids, gate_scores, experts_all):
    row_count = expert_ids.shape[0]
    expert_axis = lax.broadcasted_iota(jnp.int32, (1, 1, experts_all), 2)
    matches = expert_ids[:, :, None] == expert_axis
    weights = gate_scores / jnp.sum(gate_scores, axis=1, keepdims=True)
    row_weight = jnp.sum(jnp.where(matches, weights[:, :, None], 0.0), axis=1).T
    routed = jnp.any(matches, axis=1).astype(jnp.bfloat16).T
    before = (
        lax.broadcasted_iota(jnp.int32, (row_count, row_count), 0)
        < lax.broadcasted_iota(jnp.int32, (row_count, row_count), 1)
    ).astype(jnp.bfloat16)
    rank = jnp.dot(routed, before, preferred_element_type=jnp.float32)
    slot = jnp.where(routed > 0, rank, -1.0).astype(jnp.int32)
    return slot, row_weight


GATE_CHUNKS = 8
DOWN_CHUNKS = 8


def experts_kernel(
    rows_ref, gain_ref, gate_hbm, up_hbm, down_hbm, out_ref,
    gate_ref, up_ref, down_ref, normed_ref, gate_sum, up_sum, act_ref, gate_sem, up_sem, down_sem,
):
    replicas, pieces, slots, chunk = rows_ref.shape
    total = replicas * slots
    width = pieces * chunk
    depth = width // GATE_CHUNKS
    span = width // DOWN_CHUNKS

    def gate_copies(i):
        rows = pl.ds(i * depth, depth)
        return (
            pltpu.make_async_copy(gate_hbm.at[rows, :], gate_ref.at[rows, :], gate_sem.at[i]),
            pltpu.make_async_copy(up_hbm.at[rows, :], up_ref.at[rows, :], up_sem.at[i]),
        )

    def down_copy(i):
        columns = pl.ds(i * span, span)
        return pltpu.make_async_copy(
            down_hbm.at[:, columns], down_ref.at[:, columns], down_sem.at[i]
        )

    for i in range(GATE_CHUNKS):
        for copy in gate_copies(i):
            copy.start()
    for i in range(DOWN_CHUNKS):
        down_copy(i).start()

    squares = jnp.zeros((total, chunk), jnp.float32)
    for piece in range(pieces):
        part = rows_ref[:, piece].reshape(total, chunk).astype(jnp.float32)
        squares = squares + part * part
    spread = jnp.sum(squares, axis=-1, keepdims=True) * (1.0 / width)
    scale = lax.rsqrt(spread + 1e-06)
    for piece in range(pieces):
        part = rows_ref[:, piece].reshape(total, chunk).astype(jnp.float32)
        columns = pl.ds(piece * chunk, chunk)
        normed_ref[:, columns] = (part * scale * gain_ref[:, columns]).astype(jnp.bfloat16)

    for i in range(GATE_CHUNKS):
        rows = pl.ds(i * depth, depth)
        for copy in gate_copies(i):
            copy.wait()
        part = normed_ref[:, rows]
        gate_part = jnp.dot(part, gate_ref[rows, :], preferred_element_type=jnp.float32)
        up_part = jnp.dot(part, up_ref[rows, :], preferred_element_type=jnp.float32)
        if i == 0:
            gate_sum[...] = gate_part
            up_sum[...] = up_part
        else:
            gate_sum[...] += gate_part
            up_sum[...] += up_part
    gates = gate_sum[...]
    act_ref[...] = (gates / (1.0 + jnp.exp(-gates)) * up_sum[...]).astype(jnp.bfloat16)

    per_copy = span // chunk
    for piece in range(pieces):
        if piece % per_copy == 0:
            down_copy(piece // per_copy).wait()
        columns = pl.ds(piece * chunk, chunk)
        part = jnp.dot(act_ref[...], down_ref[:, columns], preferred_element_type=jnp.float32)
        out_ref[:, piece] = part.astype(jnp.bfloat16).reshape(replicas, slots, chunk)


def run_experts(rows, norm_gain, w_gate, w_up, w_down):
    replicas, pieces, slots, chunk = rows.shape
    width, hidden_units = w_gate.shape
    total = replicas * slots
    whole = pl.BlockSpec(memory_space=pltpu.VMEM)
    left = pl.BlockSpec(memory_space=pl.ANY)
    return pl.pallas_call(
        experts_kernel,
        out_shape=jax.ShapeDtypeStruct(rows.shape, jnp.bfloat16),
        in_specs=[whole, whole, left, left, left],
        out_specs=whole,
        scratch_shapes=[
            pltpu.VMEM((width, hidden_units), jnp.bfloat16),
            pltpu.VMEM((width, hidden_units), jnp.bfloat16),
            pltpu.VMEM((hidden_units, width), jnp.bfloat16),
            pltpu.VMEM((total, width), jnp.bfloat16),
            pltpu.VMEM((total, hidden_units), jnp.float32),
            pltpu.VMEM((total, hidden_units), jnp.float32),
            pltpu.VMEM((total, hidden_units), jnp.bfloat16),
            pltpu.SemaphoreType.DMA((GATE_CHUNKS,)),
            pltpu.SemaphoreType.DMA((GATE_CHUNKS,)),
            pltpu.SemaphoreType.DMA((DOWN_CHUNKS,)),
        ],
        compiler_params=pltpu.CompilerParams(vmem_limit_bytes=48 * 1024 * 1024),
        name="experts",
    )(rows, norm_gain.reshape(1, width), w_gate, w_up, w_down)


def shards(
    residual_in,
    query,
    fresh_key,
    fresh_value,
    key_cache,
    value_cache,
    lengths,
    out_weight,
    norm_gain,
    expert_ids,
    gate_scores,
    w_gate,
    w_up,
    w_down,
):
    both = ("dp", "tensor")
    row_count, width = residual_in.shape
    tensor_width = lax.axis_size("tensor")
    replica_count = lax.axis_size("dp")
    experts_all = replica_count * tensor_width
    column = lax.axis_index("tensor")
    chunk = width // tensor_width
    cap_slots = 2 * max(1, row_count * expert_ids.shape[1] // experts_all)

    heads_out = attend(
        query, fresh_key, fresh_value, key_cache, value_cache, lengths, column, tensor_width
    )
    partial = jnp.einsum(
        "rk,ktj->trj",
        heads_out,
        out_weight.reshape(-1, tensor_width, chunk),
        preferred_element_type=jnp.float32,
    ).astype(jnp.bfloat16)
    pieces = lax.all_to_all(partial, "tensor", split_axis=0, concat_axis=0, tiled=True)
    proj = jnp.sum(pieces.astype(jnp.float32), axis=0)
    residual = lax.dynamic_slice_in_dim(residual_in, column * chunk, chunk, 1)
    hidden = (residual.astype(jnp.float32) + proj).astype(jnp.bfloat16)

    slot, row_weight = route(expert_ids, gate_scores, experts_all)
    slot_axis = lax.broadcasted_iota(jnp.int32, (1, cap_slots, 1), 1)
    chosen = slot[:, None, :] == slot_axis
    outgoing = jnp.einsum(
        "esr,rj->esj", chosen.astype(jnp.bfloat16), hidden, preferred_element_type=jnp.float32
    ).astype(jnp.bfloat16)
    received = lax.all_to_all(outgoing, both, split_axis=0, concat_axis=0, tiled=True)

    rows = received.reshape(replica_count, tensor_width, cap_slots, chunk)
    answered = run_experts(rows, norm_gain, w_gate[0], w_up[0], w_down[0])
    answered = answered.reshape(experts_all, cap_slots, chunk)
    returned = lax.all_to_all(answered, both, split_axis=0, concat_axis=0, tiled=True)

    spread_weight = jnp.where(chosen, row_weight[:, None, :], 0.0)
    coarse = spread_weight.astype(jnp.bfloat16)
    fine = (spread_weight - coarse.astype(jnp.float32)).astype(jnp.bfloat16)
    mixture = jnp.einsum(
        "esr,esj->rj", coarse, returned, preferred_element_type=jnp.float32
    ) + jnp.einsum("esr,esj->rj", fine, returned, preferred_element_type=jnp.float32)
    layer = (hidden.astype(jnp.float32) + mixture).astype(jnp.bfloat16)
    own = lax.all_to_all(
        layer.reshape(tensor_width, row_count // tensor_width, chunk),
        "tensor",
        split_axis=0,
        concat_axis=0,
        tiled=True,
    )
    return own.transpose(1, 0, 2).reshape(row_count // tensor_width, width)


def solution(mesh):
    placed = (
        P("dp", None),
        P("dp", "tensor"),
        P("dp", None, None),
        P("dp", None, None),
        P("dp", "tensor", None, None),
        P("dp", "tensor", None, None),
        P("dp"),
        P("tensor", None),
        P(),
        P("dp", None),
        P("dp", None),
        P(("dp", "tensor"), None, None),
        P(("dp", "tensor"), None, None),
        P(("dp", "tensor"), None, None),
    )
    return jax.shard_map(
        shards, mesh=mesh, in_specs=placed, out_specs=P(("dp", "tensor"), None), check_vma=False
    )
```

```python
import jax
import jax.numpy as jnp
from jax import lax
from jax.experimental import pallas as pl
from jax.experimental.pallas import tpu as pltpu
from jax.sharding import PartitionSpec as P


ROWS_STEP = 32
STEPS_AHEAD = 3
WEIGHT_COPIES = 4


def attend_kernel(
    head_ref, lengths_hbm, query_hbm, fresh_key_hbm, fresh_value_hbm, key_hbm, value_hbm, weight_hbm,
    out_ref,
    lengths_ref, query_ref, fresh_key_ref, fresh_value_ref, key_ref, value_ref, weight_ref,
    query_scr, own_key_scr, own_value_scr, attended_scr, heads_scr,
    small_sem, key_sem, value_sem, weight_sem,
):
    row_count, positions, head_size = key_ref.shape
    head_count = query_ref.shape[1] // head_size
    pieces, _, chunk = out_ref.shape
    steps = row_count // ROWS_STEP
    width = weight_ref.shape[0] // WEIGHT_COPIES
    score_scale = head_size ** (-0.5)

    def cache_copies(step):
        rows = pl.ds(step * ROWS_STEP, ROWS_STEP)
        return (
            pltpu.make_async_copy(key_hbm.at[rows], key_ref.at[rows], key_sem.at[step]),
            pltpu.make_async_copy(value_hbm.at[rows], value_ref.at[rows], value_sem.at[step]),
        )

    def weight_copy(i):
        rows = pl.ds(i * width, width)
        return pltpu.make_async_copy(weight_hbm.at[rows], weight_ref.at[rows], weight_sem.at[i])

    small = [
        pltpu.make_async_copy(query_hbm, query_ref, small_sem.at[0]),
        pltpu.make_async_copy(fresh_key_hbm, fresh_key_ref, small_sem.at[1]),
        pltpu.make_async_copy(fresh_value_hbm, fresh_value_ref, small_sem.at[2]),
        pltpu.make_async_copy(lengths_hbm, lengths_ref, small_sem.at[3]),
    ]
    for copy in small:
        copy.start()
    for step in range(STEPS_AHEAD):
        for copy in cache_copies(step):
            copy.start()
    for copy in small:
        copy.wait()

    group = lax.broadcasted_iota(jnp.int32, fresh_key_ref.shape, 1) == head_ref[0]
    own_key = jnp.sum(jnp.where(group, fresh_key_ref[...].astype(jnp.float32), 0.0), axis=1)
    own_value = jnp.sum(jnp.where(group, fresh_value_ref[...].astype(jnp.float32), 0.0), axis=1)
    for head in range(head_count):
        rows = pl.ds(head, row_count, stride=head_count)
        columns = pl.ds(head * head_size, head_size)
        query_scr[rows, :] = query_ref[:, columns].astype(jnp.float32)
        own_key_scr[rows, :] = own_key
        own_value_scr[rows, :] = own_value

    pair = 2 * head_count
    upper = lax.broadcasted_iota(jnp.int32, (pair, positions), 0) < head_count
    position = lax.broadcasted_iota(jnp.int32, (pair, positions), 1)

    @pl.loop(0, steps)
    def _(step):
        for copy in cache_copies(step):
            copy.wait()

        @pl.when(step + STEPS_AHEAD < steps)
        def _():
            for copy in cache_copies(step + STEPS_AHEAD):
                copy.start()

        @pl.when(step + WEIGHT_COPIES >= steps)
        def _():
            weight_copy(step + WEIGHT_COPIES - steps).start()

        first = pl.multiple_of(step * (ROWS_STEP * head_count), ROWS_STEP * head_count)
        queries = query_scr[pl.ds(first, ROWS_STEP * head_count), :]
        parts = []
        for i in range(ROWS_STEP // 2):
            row = step * ROWS_STEP + 2 * i
            keys = key_ref[pl.ds(row, 2)].reshape(2 * positions, head_size)
            asked = queries[i * pair : (i + 1) * pair].astype(jnp.bfloat16)
            both = lax.dot_general(
                asked, keys, (((1,), (1,)), ((), ())), preferred_element_type=jnp.float32
            )
            scores = jnp.where(upper, both[:, :positions], both[:, positions:]) * score_scale
            live = jnp.where(upper, lengths_ref[row], lengths_ref[row + 1])
            parts.append(jnp.where(position < live, scores, -1e30))
        scores = jnp.concatenate(parts, axis=0)
        own_keys = own_key_scr[pl.ds(first, ROWS_STEP * head_count), :]
        own_score = jnp.sum(queries * own_keys, axis=-1, keepdims=True) * score_scale
        row_max = jnp.maximum(jnp.max(scores, axis=-1, keepdims=True), own_score)
        terms = jnp.exp(scores - row_max)
        own_term = jnp.exp(own_score - row_max)
        total = jnp.sum(terms, axis=-1, keepdims=True) + own_term
        probs = (terms / total).astype(jnp.bfloat16).astype(jnp.float32)
        own_prob = (own_term / total).astype(jnp.bfloat16).astype(jnp.float32)
        parts = []
        for i in range(ROWS_STEP // 2):
            row = step * ROWS_STEP + 2 * i
            values = value_ref[pl.ds(row, 2)].reshape(2 * positions, head_size)
            prob = probs[i * pair : (i + 1) * pair]
            spread = jnp.concatenate(
                [jnp.where(upper, prob, 0.0), jnp.where(upper, 0.0, prob)], axis=1
            ).astype(jnp.bfloat16)
            parts.append(jnp.dot(spread, values, preferred_element_type=jnp.float32))
        attended = jnp.concatenate(parts, axis=0)
        own_values = own_value_scr[pl.ds(first, ROWS_STEP * head_count), :]
        attended_scr[pl.ds(first, ROWS_STEP * head_count), :] = attended + own_prob * own_values

    for head in range(head_count):
        columns = pl.ds(head * head_size, head_size)
        rows = pl.ds(head, row_count, stride=head_count)
        heads_scr[:, columns] = attended_scr[rows, :].astype(jnp.bfloat16)
    for i in range(WEIGHT_COPIES):
        weight_copy(i).wait()
    for piece in range(pieces):
        columns = pl.ds(piece * chunk, chunk)
        part = jnp.dot(
            heads_scr[...], weight_ref[:, columns], preferred_element_type=jnp.float32
        )
        out_ref[piece] = part.astype(jnp.bfloat16)


def run_attend(query, fresh_key, fresh_value, key_cache, value_cache, lengths, kv_head, out_weight, pieces):
    row_count, positions, head_size = key_cache.shape
    width = out_weight.shape[1]
    many = query.shape[0] * query.shape[1] // head_size
    whole = pl.BlockSpec(memory_space=pltpu.VMEM)
    scalars = pl.BlockSpec(memory_space=pltpu.SMEM)
    left = pl.BlockSpec(memory_space=pltpu.HBM)
    steps = row_count // ROWS_STEP
    return pl.pallas_call(
        attend_kernel,
        out_shape=jax.ShapeDtypeStruct((pieces, row_count, width // pieces), jnp.bfloat16),
        in_specs=[scalars] + [left] * 7,
        out_specs=whole,
        scratch_shapes=[
            pltpu.SMEM(lengths.shape, jnp.int32),
            pltpu.VMEM(query.shape, jnp.bfloat16),
            pltpu.VMEM(fresh_key.shape, jnp.bfloat16),
            pltpu.VMEM(fresh_value.shape, jnp.bfloat16),
            pltpu.VMEM(key_cache.shape, jnp.bfloat16),
            pltpu.VMEM(value_cache.shape, jnp.bfloat16),
            pltpu.VMEM(out_weight.shape, jnp.bfloat16),
            pltpu.VMEM((many, head_size), jnp.float32),
            pltpu.VMEM((many, head_size), jnp.float32),
            pltpu.VMEM((many, head_size), jnp.float32),
            pltpu.VMEM((many, head_size), jnp.float32),
            pltpu.VMEM(query.shape, jnp.bfloat16),
            pltpu.SemaphoreType.DMA((4,)),
            pltpu.SemaphoreType.DMA((steps,)),
            pltpu.SemaphoreType.DMA((steps,)),
            pltpu.SemaphoreType.DMA((WEIGHT_COPIES,)),
        ],
        compiler_params=pltpu.CompilerParams(vmem_limit_bytes=60 * 1024 * 1024),
        name="attend",
    )(kv_head, lengths, query, fresh_key, fresh_value, key_cache, value_cache, out_weight)


def route(expert_ids, gate_scores, experts_all):
    row_count = expert_ids.shape[0]
    expert_axis = lax.broadcasted_iota(jnp.int32, (1, 1, experts_all), 2)
    matches = expert_ids[:, :, None] == expert_axis
    weights = gate_scores / jnp.sum(gate_scores, axis=1, keepdims=True)
    row_weight = jnp.sum(jnp.where(matches, weights[:, :, None], 0.0), axis=1).T
    routed = jnp.any(matches, axis=1).astype(jnp.bfloat16).T
    before = (
        lax.broadcasted_iota(jnp.int32, (row_count, row_count), 0)
        < lax.broadcasted_iota(jnp.int32, (row_count, row_count), 1)
    ).astype(jnp.bfloat16)
    rank = jnp.dot(routed, before, preferred_element_type=jnp.float32)
    slot = jnp.where(routed > 0, rank, -1.0).astype(jnp.int32)
    return slot, row_weight


UNIT_CHUNK = 256
DOWN_CHUNKS = 4
COPIES_AHEAD = 6


def experts_kernel(
    rows_ref, gain_ref, gate_hbm, up_hbm, down_hbm, out_ref,
    gate_ref, up_ref, down_ref, normed_ref, act_ref, gate_sem, up_sem, down_sem,
):
    replicas, pieces, slots, chunk = rows_ref.shape
    total = replicas * slots
    width = pieces * chunk
    unit_chunks = gate_ref.shape[1] // UNIT_CHUNK
    span = width // DOWN_CHUNKS

    def unit_copies(i):
        units = pl.ds(i * UNIT_CHUNK, UNIT_CHUNK)
        return (
            pltpu.make_async_copy(gate_hbm.at[:, units], gate_ref.at[:, units], gate_sem.at[i]),
            pltpu.make_async_copy(up_hbm.at[:, units], up_ref.at[:, units], up_sem.at[i]),
        )

    def down_copy(i):
        columns = pl.ds(i * span, span)
        return pltpu.make_async_copy(
            down_hbm.at[:, columns], down_ref.at[:, columns], down_sem.at[i]
        )

    order = [copy for i in range(unit_chunks) for copy in unit_copies(i)]
    order += [down_copy(i) for i in range(DOWN_CHUNKS)]
    for copy in order[:COPIES_AHEAD]:
        copy.start()

    def take(i):
        order[i].wait()
        if i + COPIES_AHEAD < len(order):
            order[i + COPIES_AHEAD].start()

    squares = jnp.zeros((total, chunk), jnp.float32)
    for piece in range(pieces):
        part = rows_ref[:, piece].reshape(total, chunk).astype(jnp.float32)
        squares = squares + part * part
    spread = jnp.sum(squares, axis=-1, keepdims=True) * (1.0 / width)
    scale = lax.rsqrt(spread + 1e-06)
    for piece in range(pieces):
        part = rows_ref[:, piece].reshape(total, chunk).astype(jnp.float32)
        columns = pl.ds(piece * chunk, chunk)
        normed_ref[:, columns] = (part * scale * gain_ref[:, columns]).astype(jnp.bfloat16)

    for i in range(unit_chunks):
        units = pl.ds(i * UNIT_CHUNK, UNIT_CHUNK)
        take(2 * i)
        gates = jnp.dot(normed_ref[...], gate_ref[:, units], preferred_element_type=jnp.float32)
        take(2 * i + 1)
        ups = jnp.dot(normed_ref[...], up_ref[:, units], preferred_element_type=jnp.float32)
        act_ref[:, units] = (gates / (1.0 + jnp.exp(-gates)) * ups).astype(jnp.bfloat16)

    per_copy = span // chunk
    for piece in range(pieces):
        if piece % per_copy == 0:
            take(2 * unit_chunks + piece // per_copy)
        columns = pl.ds(piece * chunk, chunk)
        part = jnp.dot(act_ref[...], down_ref[:, columns], preferred_element_type=jnp.float32)
        out_ref[:, piece] = part.astype(jnp.bfloat16).reshape(replicas, slots, chunk)


def run_experts(rows, norm_gain, w_gate, w_up, w_down):
    replicas, pieces, slots, chunk = rows.shape
    width, hidden_units = w_gate.shape
    total = replicas * slots
    unit_chunks = hidden_units // UNIT_CHUNK
    whole = pl.BlockSpec(memory_space=pltpu.VMEM)
    left = pl.BlockSpec(memory_space=pltpu.HBM)
    return pl.pallas_call(
        experts_kernel,
        out_shape=jax.ShapeDtypeStruct(rows.shape, jnp.bfloat16),
        in_specs=[whole, whole, left, left, left],
        out_specs=whole,
        scratch_shapes=[
            pltpu.VMEM((width, hidden_units), jnp.bfloat16),
            pltpu.VMEM((width, hidden_units), jnp.bfloat16),
            pltpu.VMEM((hidden_units, width), jnp.bfloat16),
            pltpu.VMEM((total, width), jnp.bfloat16),
            pltpu.VMEM((total, hidden_units), jnp.bfloat16),
            pltpu.SemaphoreType.DMA((unit_chunks,)),
            pltpu.SemaphoreType.DMA((unit_chunks,)),
            pltpu.SemaphoreType.DMA((DOWN_CHUNKS,)),
        ],
        compiler_params=pltpu.CompilerParams(vmem_limit_bytes=60 * 1024 * 1024),
        name="experts",
    )(rows, norm_gain.reshape(1, width), w_gate, w_up, w_down)


def shards(
    residual_in,
    query,
    fresh_key,
    fresh_value,
    key_cache,
    value_cache,
    lengths,
    out_weight,
    norm_gain,
    expert_ids,
    gate_scores,
    w_gate,
    w_up,
    w_down,
):
    both = ("dp", "tensor")
    row_count, width = residual_in.shape
    tensor_width = lax.axis_size("tensor")
    replica_count = lax.axis_size("dp")
    experts_all = replica_count * tensor_width
    column = lax.axis_index("tensor")
    chunk = width // tensor_width
    cap_slots = 2 * max(1, row_count * expert_ids.shape[1] // experts_all)

    kv_head = (column // (tensor_width // fresh_key.shape[1])).astype(jnp.int32).reshape(1)
    partial = run_attend(
        query, fresh_key, fresh_value, key_cache[:, 0], value_cache[:, 0], lengths, kv_head,
        out_weight, tensor_width,
    )
    pieces = lax.all_to_all(partial, "tensor", split_axis=0, concat_axis=0, tiled=True)
    proj = jnp.sum(pieces.astype(jnp.float32), axis=0)
    residual = lax.dynamic_slice_in_dim(residual_in, column * chunk, chunk, 1)
    hidden = (residual.astype(jnp.float32) + proj).astype(jnp.bfloat16)

    slot, row_weight = route(expert_ids, gate_scores, experts_all)
    slot_axis = lax.broadcasted_iota(jnp.int32, (1, cap_slots, 1), 1)
    chosen = slot[:, None, :] == slot_axis
    outgoing = jnp.einsum(
        "esr,rj->esj", chosen.astype(jnp.bfloat16), hidden, preferred_element_type=jnp.float32
    ).astype(jnp.bfloat16)
    received = lax.all_to_all(outgoing, both, split_axis=0, concat_axis=0, tiled=True)

    rows = received.reshape(replica_count, tensor_width, cap_slots, chunk)
    answered = run_experts(rows, norm_gain, w_gate[0], w_up[0], w_down[0])
    answered = answered.reshape(experts_all, cap_slots, chunk)
    returned = lax.all_to_all(answered, both, split_axis=0, concat_axis=0, tiled=True)

    spread_weight = jnp.where(chosen, row_weight[:, None, :], 0.0)
    coarse = spread_weight.astype(jnp.bfloat16)
    fine = (spread_weight - coarse.astype(jnp.float32)).astype(jnp.bfloat16)
    mixture = jnp.einsum(
        "esr,esj->rj", coarse, returned, preferred_element_type=jnp.float32
    ) + jnp.einsum("esr,esj->rj", fine, returned, preferred_element_type=jnp.float32)
    layer = (hidden.astype(jnp.float32) + mixture).astype(jnp.bfloat16)
    own = lax.all_to_all(
        layer.reshape(tensor_width, row_count // tensor_width, chunk),
        "tensor",
        split_axis=0,
        concat_axis=0,
        tiled=True,
    )
    return own.transpose(1, 0, 2).reshape(row_count // tensor_width, width)


def solution(mesh):
    placed = (
        P("dp", None),
        P("dp", "tensor"),
        P("dp", None, None),
        P("dp", None, None),
        P("dp", "tensor", None, None),
        P("dp", "tensor", None, None),
        P("dp"),
        P("tensor", None),
        P(),
        P("dp", None),
        P("dp", None),
        P(("dp", "tensor"), None, None),
        P(("dp", "tensor"), None, None),
        P(("dp", "tensor"), None, None),
    )
    return jax.shard_map(
        shards, mesh=mesh, in_specs=placed, out_specs=P(("dp", "tensor"), None), check_vma=False
    )
```

```python
import jax
import jax.numpy as jnp
from jax import lax
from jax.experimental import pallas as pl
from jax.experimental.pallas import tpu as pltpu
from jax.sharding import PartitionSpec as P


ROWS_STEP = 32
STEPS_AHEAD = 3
WEIGHT_COPIES = 4


def attend_kernel(
    head_ref, lengths_hbm, query_hbm, fresh_key_hbm, fresh_value_hbm, key_hbm, value_hbm, weight_hbm,
    out_ref,
    lengths_ref, query_ref, fresh_key_ref, fresh_value_ref, key_ref, value_ref, weight_ref,
    query_scr, own_key_scr, own_value_scr, attended_scr, heads_scr,
    small_sem, key_sem, value_sem, weight_sem,
):
    row_count, positions, head_size = key_ref.shape
    head_count = query_ref.shape[1] // head_size
    pieces, _, chunk = out_ref.shape
    steps = row_count // ROWS_STEP
    width = weight_ref.shape[0] // WEIGHT_COPIES
    score_scale = head_size ** (-0.5)

    def cache_copies(step):
        rows = pl.ds(step * ROWS_STEP, ROWS_STEP)
        return (
            pltpu.make_async_copy(key_hbm.at[rows], key_ref.at[rows], key_sem.at[step]),
            pltpu.make_async_copy(value_hbm.at[rows], value_ref.at[rows], value_sem.at[step]),
        )

    def weight_copy(i):
        rows = pl.ds(i * width, width)
        return pltpu.make_async_copy(weight_hbm.at[rows], weight_ref.at[rows], weight_sem.at[i])

    small = [
        pltpu.make_async_copy(query_hbm, query_ref, small_sem.at[0]),
        pltpu.make_async_copy(fresh_key_hbm, fresh_key_ref, small_sem.at[1]),
        pltpu.make_async_copy(fresh_value_hbm, fresh_value_ref, small_sem.at[2]),
        pltpu.make_async_copy(lengths_hbm, lengths_ref, small_sem.at[3]),
    ]
    for copy in small:
        copy.start()
    for step in range(STEPS_AHEAD):
        for copy in cache_copies(step):
            copy.start()
    for copy in small:
        copy.wait()

    group = lax.broadcasted_iota(jnp.int32, fresh_key_ref.shape, 1) == head_ref[0]
    own_key = jnp.sum(jnp.where(group, fresh_key_ref[...].astype(jnp.float32), 0.0), axis=1)
    own_value = jnp.sum(jnp.where(group, fresh_value_ref[...].astype(jnp.float32), 0.0), axis=1)
    for head in range(head_count):
        rows = pl.ds(head, row_count, stride=head_count)
        columns = pl.ds(head * head_size, head_size)
        query_scr[rows, :] = query_ref[:, columns].astype(jnp.float32)
        own_key_scr[rows, :] = own_key
        own_value_scr[rows, :] = own_value

    pair = 2 * head_count
    upper = lax.broadcasted_iota(jnp.int32, (pair, positions), 0) < head_count
    position = lax.broadcasted_iota(jnp.int32, (pair, positions), 1)

    @pl.loop(0, steps)
    def _(step):
        for copy in cache_copies(step):
            copy.wait()

        @pl.when(step + STEPS_AHEAD < steps)
        def _():
            for copy in cache_copies(step + STEPS_AHEAD):
                copy.start()

        @pl.when(step + WEIGHT_COPIES >= steps)
        def _():
            weight_copy(step + WEIGHT_COPIES - steps).start()

        first = pl.multiple_of(step * (ROWS_STEP * head_count), ROWS_STEP * head_count)
        queries = query_scr[pl.ds(first, ROWS_STEP * head_count), :]
        parts = []
        for i in range(ROWS_STEP // 2):
            row = step * ROWS_STEP + 2 * i
            keys = key_ref[pl.ds(row, 2)].reshape(2 * positions, head_size)
            asked = queries[i * pair : (i + 1) * pair].astype(jnp.bfloat16)
            both = lax.dot_general(
                asked, keys, (((1,), (1,)), ((), ())), preferred_element_type=jnp.float32
            )
            scores = jnp.where(upper, both[:, :positions], both[:, positions:]) * score_scale
            live = jnp.where(upper, lengths_ref[row], lengths_ref[row + 1])
            parts.append(jnp.where(position < live, scores, -1e30))
        scores = jnp.concatenate(parts, axis=0)
        own_keys = own_key_scr[pl.ds(first, ROWS_STEP * head_count), :]
        own_score = jnp.sum(queries * own_keys, axis=-1, keepdims=True) * score_scale
        row_max = jnp.maximum(jnp.max(scores, axis=-1, keepdims=True), own_score)
        terms = jnp.exp(scores - row_max)
        own_term = jnp.exp(own_score - row_max)
        total = jnp.sum(terms, axis=-1, keepdims=True) + own_term
        probs = (terms / total).astype(jnp.bfloat16).astype(jnp.float32)
        own_prob = (own_term / total).astype(jnp.bfloat16).astype(jnp.float32)
        parts = []
        for i in range(ROWS_STEP // 2):
            row = step * ROWS_STEP + 2 * i
            values = value_ref[pl.ds(row, 2)].reshape(2 * positions, head_size)
            prob = probs[i * pair : (i + 1) * pair]
            spread = jnp.concatenate(
                [jnp.where(upper, prob, 0.0), jnp.where(upper, 0.0, prob)], axis=1
            ).astype(jnp.bfloat16)
            parts.append(jnp.dot(spread, values, preferred_element_type=jnp.float32))
        attended = jnp.concatenate(parts, axis=0)
        own_values = own_value_scr[pl.ds(first, ROWS_STEP * head_count), :]
        attended_scr[pl.ds(first, ROWS_STEP * head_count), :] = attended + own_prob * own_values

    for head in range(head_count):
        columns = pl.ds(head * head_size, head_size)
        rows = pl.ds(head, row_count, stride=head_count)
        heads_scr[:, columns] = attended_scr[rows, :].astype(jnp.bfloat16)
    for i in range(WEIGHT_COPIES):
        weight_copy(i).wait()
    for piece in range(pieces):
        columns = pl.ds(piece * chunk, chunk)
        part = jnp.dot(
            heads_scr[...], weight_ref[:, columns], preferred_element_type=jnp.float32
        )
        out_ref[piece] = part.astype(jnp.bfloat16)


def run_attend(query, fresh_key, fresh_value, key_cache, value_cache, lengths, kv_head, out_weight, pieces):
    row_count, positions, head_size = key_cache.shape
    width = out_weight.shape[1]
    many = query.shape[0] * query.shape[1] // head_size
    whole = pl.BlockSpec(memory_space=pltpu.VMEM)
    scalars = pl.BlockSpec(memory_space=pltpu.SMEM)
    left = pl.BlockSpec(memory_space=pltpu.HBM)
    steps = row_count // ROWS_STEP
    return pl.pallas_call(
        attend_kernel,
        out_shape=jax.ShapeDtypeStruct((pieces, row_count, width // pieces), jnp.bfloat16),
        in_specs=[scalars] + [left] * 7,
        out_specs=whole,
        scratch_shapes=[
            pltpu.SMEM(lengths.shape, jnp.int32),
            pltpu.VMEM(query.shape, jnp.bfloat16),
            pltpu.VMEM(fresh_key.shape, jnp.bfloat16),
            pltpu.VMEM(fresh_value.shape, jnp.bfloat16),
            pltpu.VMEM(key_cache.shape, jnp.bfloat16),
            pltpu.VMEM(value_cache.shape, jnp.bfloat16),
            pltpu.VMEM(out_weight.shape, jnp.bfloat16),
            pltpu.VMEM((many, head_size), jnp.float32),
            pltpu.VMEM((many, head_size), jnp.float32),
            pltpu.VMEM((many, head_size), jnp.float32),
            pltpu.VMEM((many, head_size), jnp.float32),
            pltpu.VMEM(query.shape, jnp.bfloat16),
            pltpu.SemaphoreType.DMA((4,)),
            pltpu.SemaphoreType.DMA((steps,)),
            pltpu.SemaphoreType.DMA((steps,)),
            pltpu.SemaphoreType.DMA((WEIGHT_COPIES,)),
        ],
        compiler_params=pltpu.CompilerParams(vmem_limit_bytes=60 * 1024 * 1024),
        name="attend",
    )(kv_head, lengths, query, fresh_key, fresh_value, key_cache, value_cache, out_weight)


def route_kernel(column_ref, ids_ref, scores_ref, residual_hbm, slot_ref, weight_ref, residual_ref, sem):
    experts, row_count = slot_ref.shape
    chunk = residual_ref.shape[1]
    own = pl.ds(pl.multiple_of(column_ref[0] * chunk, chunk), chunk)
    copy = pltpu.make_async_copy(residual_hbm.at[:, own], residual_ref, sem)
    copy.start()
    topk = ids_ref.shape[0]
    scores = scores_ref[...]
    weights = scores / jnp.sum(scores, axis=0, keepdims=True)
    expert = lax.broadcasted_iota(jnp.int32, (experts, row_count), 0)
    named = jnp.zeros((experts, row_count), jnp.float32)
    weight = jnp.zeros((experts, row_count), jnp.float32)
    for k in range(topk):
        match = ids_ref[k : k + 1, :] == expert
        named = named + jnp.where(match, 1.0, 0.0)
        weight = weight + jnp.where(match, weights[k : k + 1, :], 0.0)
    earlier = lax.broadcasted_iota(jnp.int32, (row_count, row_count), 0)
    later = lax.broadcasted_iota(jnp.int32, (row_count, row_count), 1)
    before = jnp.where(earlier < later, 1.0, 0.0).astype(jnp.bfloat16)
    rank = jnp.dot(named.astype(jnp.bfloat16), before, preferred_element_type=jnp.float32)
    slot_ref[...] = jnp.where(named > 0.0, rank, -1.0).astype(jnp.int32)
    weight_ref[...] = weight
    copy.wait()


def run_route(column, expert_ids, gate_scores, residual_in, experts_all, chunk):
    row_count = expert_ids.shape[0]
    whole = pl.BlockSpec(memory_space=pltpu.VMEM)
    return pl.pallas_call(
        route_kernel,
        out_shape=(
            jax.ShapeDtypeStruct((experts_all, row_count), jnp.int32),
            jax.ShapeDtypeStruct((experts_all, row_count), jnp.float32),
            jax.ShapeDtypeStruct((row_count, chunk), residual_in.dtype),
        ),
        in_specs=[
            pl.BlockSpec(memory_space=pltpu.SMEM), whole, whole, pl.BlockSpec(memory_space=pl.ANY),
        ],
        out_specs=(whole, whole, whole),
        scratch_shapes=[pltpu.SemaphoreType.DMA],
        compiler_params=pltpu.CompilerParams(vmem_limit_bytes=4 * 1024 * 1024),
        name="route",
    )(column, expert_ids.T, gate_scores.T, residual_in)


def select_kernel(pieces_ref, residual_ref, slot_ref, hidden_ref, outgoing_ref):
    sources = pieces_ref.shape[0]
    experts, slots, chunk = outgoing_ref.shape
    row_count = slot_ref.shape[1]
    proj = pieces_ref[0].astype(jnp.float32)
    for source in range(1, sources):
        proj = proj + pieces_ref[source].astype(jnp.float32)
    hidden = (residual_ref[...].astype(jnp.float32) + proj).astype(jnp.bfloat16)
    hidden_ref[...] = hidden
    group = row_count // slots
    place = lax.broadcasted_iota(jnp.int32, (group, slots, row_count), 1)
    for first in range(0, experts, group):
        chosen = slot_ref[pl.ds(first, group), :][:, None, :] == place
        selector = jnp.where(chosen, 1.0, 0.0).reshape(group * slots, row_count)
        rows = jnp.dot(selector.astype(jnp.bfloat16), hidden, preferred_element_type=jnp.float32)
        outgoing_ref[pl.ds(first, group)] = rows.astype(jnp.bfloat16).reshape(group, slots, chunk)


def run_select(pieces, residual, slot, slots):
    experts, row_count = slot.shape
    chunk = pieces.shape[2]
    whole = pl.BlockSpec(memory_space=pltpu.VMEM)
    return pl.pallas_call(
        select_kernel,
        out_shape=(
            jax.ShapeDtypeStruct((row_count, chunk), jnp.bfloat16),
            jax.ShapeDtypeStruct((experts, slots, chunk), jnp.bfloat16),
        ),
        in_specs=[whole] * 3,
        out_specs=(whole, whole),
        compiler_params=pltpu.CompilerParams(vmem_limit_bytes=8 * 1024 * 1024),
        cost_estimate=pl.CostEstimate(flops=100_000_000_000, bytes_accessed=4_000_000, transcendentals=0),
        name="select",
    )(pieces, residual, slot)


def experts_kernel(rows_ref, gain_ref, gate_ref, up_ref, down_ref, out_ref, normed_ref, act_ref):
    replicas, pieces, slots, chunk = rows_ref.shape
    total = replicas * slots
    width = pieces * chunk
    squares = jnp.zeros((total, chunk), jnp.float32)
    for piece in range(pieces):
        part = rows_ref[:, piece].reshape(total, chunk).astype(jnp.float32)
        squares = squares + part * part
    spread = jnp.sum(squares, axis=-1, keepdims=True) * (1.0 / width)
    scale = lax.rsqrt(spread + 1e-06)
    for piece in range(pieces):
        part = rows_ref[:, piece].reshape(total, chunk).astype(jnp.float32)
        columns = pl.ds(piece * chunk, chunk)
        normed_ref[:, columns] = (part * scale * gain_ref[:, columns]).astype(jnp.bfloat16)
    for first in range(0, gate_ref.shape[1], chunk):
        units = pl.ds(first, chunk)
        gate_part = jnp.dot(normed_ref[...], gate_ref[:, units], preferred_element_type=jnp.float32)
        up_part = jnp.dot(normed_ref[...], up_ref[:, units], preferred_element_type=jnp.float32)
        act_ref[:, units] = (gate_part / (1.0 + jnp.exp(-gate_part)) * up_part).astype(jnp.bfloat16)
    for piece in range(pieces):
        columns = pl.ds(piece * chunk, chunk)
        part = jnp.dot(act_ref[...], down_ref[:, columns], preferred_element_type=jnp.float32)
        out_ref[:, piece] = part.astype(jnp.bfloat16).reshape(replicas, slots, chunk)


def run_experts(rows, norm_gain, weights):
    replicas, pieces, slots, chunk = rows.shape
    width, hidden_units = weights[0].shape
    total = replicas * slots
    whole = pl.BlockSpec(memory_space=pltpu.VMEM)
    return pl.pallas_call(
        experts_kernel,
        out_shape=jax.ShapeDtypeStruct(rows.shape, jnp.bfloat16),
        in_specs=[whole] * 5,
        out_specs=whole,
        scratch_shapes=[
            pltpu.VMEM((total, width), jnp.bfloat16),
            pltpu.VMEM((total, hidden_units), jnp.bfloat16),
        ],
        compiler_params=pltpu.CompilerParams(vmem_limit_bytes=16 * 1024 * 1024),
        name="experts",
    )(rows, norm_gain.reshape(1, width), *weights)


def shards(
    residual_in,
    query,
    fresh_key,
    fresh_value,
    key_cache,
    value_cache,
    lengths,
    out_weight,
    norm_gain,
    expert_ids,
    gate_scores,
    w_gate,
    w_up,
    w_down,
):
    both = ("dp", "tensor")
    row_count, width = residual_in.shape
    tensor_width = lax.axis_size("tensor")
    replica_count = lax.axis_size("dp")
    experts_all = replica_count * tensor_width
    column = lax.axis_index("tensor")
    chunk = width // tensor_width
    cap_slots = 2 * max(1, row_count * expert_ids.shape[1] // experts_all)

    kv_head = (column // (tensor_width // fresh_key.shape[1])).astype(jnp.int32).reshape(1)
    partial = run_attend(
        query, fresh_key, fresh_value, key_cache[:, 0], value_cache[:, 0], lengths, kv_head,
        out_weight, tensor_width,
    )
    pieces = lax.all_to_all(partial, "tensor", split_axis=0, concat_axis=0, tiled=True)
    own_column = column.astype(jnp.int32).reshape(1)
    slot, row_weight, residual = run_route(
        own_column, expert_ids, gate_scores, residual_in, experts_all, chunk
    )
    hidden, outgoing = run_select(pieces, residual, slot, cap_slots)
    received = lax.all_to_all(outgoing, both, split_axis=0, concat_axis=0, tiled=True)

    weights = [w_gate[0], w_up[0], w_down[0]]
    rows = received.reshape(replica_count, tensor_width, cap_slots, chunk)
    answered = run_experts(rows, norm_gain, weights)
    answered = answered.reshape(experts_all, cap_slots, chunk)
    returned = lax.all_to_all(answered, both, split_axis=0, concat_axis=0, tiled=True)

    slot_axis = lax.broadcasted_iota(jnp.int32, (1, cap_slots, 1), 1)
    chosen = slot[:, None, :] == slot_axis
    spread_weight = jnp.where(chosen, row_weight[:, None, :], 0.0)
    coarse = spread_weight.astype(jnp.bfloat16)
    fine = (spread_weight - coarse.astype(jnp.float32)).astype(jnp.bfloat16)
    mixture = jnp.einsum(
        "esr,esj->rj", coarse, returned, preferred_element_type=jnp.float32
    ) + jnp.einsum("esr,esj->rj", fine, returned, preferred_element_type=jnp.float32)
    layer = (hidden.astype(jnp.float32) + mixture).astype(jnp.bfloat16)
    own = lax.all_to_all(
        layer.reshape(tensor_width, row_count // tensor_width, chunk),
        "tensor",
        split_axis=0,
        concat_axis=0,
        tiled=True,
    )
    return own.transpose(1, 0, 2).reshape(row_count // tensor_width, width)


def solution(mesh):
    placed = (
        P("dp", None),
        P("dp", "tensor"),
        P("dp", None, None),
        P("dp", None, None),
        P("dp", "tensor", None, None),
        P("dp", "tensor", None, None),
        P("dp"),
        P("tensor", None),
        P(),
        P("dp", None),
        P("dp", None),
        P(("dp", "tensor"), None, None),
        P(("dp", "tensor"), None, None),
        P(("dp", "tensor"), None, None),
    )
    return jax.shard_map(
        shards, mesh=mesh, in_specs=placed, out_specs=P(("dp", "tensor"), None), check_vma=False
    )
```

```python
import jax
import jax.numpy as jnp
from jax import lax
from jax.experimental import pallas as pl
from jax.experimental.pallas import tpu as pltpu
from jax.sharding import PartitionSpec as P


ROWS_STEP = 32
STEPS_AHEAD = 3


def attend_kernel(
    head_ref, column_ref, lengths_hbm, residual_hbm, query_hbm, fresh_key_hbm, fresh_value_hbm, key_hbm, value_hbm, weight_hbm,
    out_ref, residual_ref,
    lengths_ref, query_ref, fresh_key_ref, fresh_value_ref, key_ref, value_ref, weight_ref,
    query_scr, own_key_scr, own_value_scr, attended_scr, heads_scr,
    small_sem, residual_sem, key_sem, value_sem, weight_sem,
):
    row_count, positions, head_size = key_ref.shape
    head_count = query_ref.shape[1] // head_size
    pieces, _, chunk = out_ref.shape
    steps = row_count // ROWS_STEP
    score_scale = head_size ** (-0.5)

    def cache_copies(step):
        rows = pl.ds(step * ROWS_STEP, ROWS_STEP)
        return (
            pltpu.make_async_copy(key_hbm.at[rows], key_ref.at[rows], key_sem.at[step]),
            pltpu.make_async_copy(value_hbm.at[rows], value_ref.at[rows], value_sem.at[step]),
        )

    weight_copy = pltpu.make_async_copy(weight_hbm, weight_ref, weight_sem)
    own = pl.ds(pl.multiple_of(column_ref[0] * chunk, chunk), chunk)
    residual_copy = pltpu.make_async_copy(residual_hbm.at[:, own], residual_ref, residual_sem)
    small = [
        pltpu.make_async_copy(query_hbm, query_ref, small_sem.at[0]),
        pltpu.make_async_copy(fresh_key_hbm, fresh_key_ref, small_sem.at[1]),
        pltpu.make_async_copy(fresh_value_hbm, fresh_value_ref, small_sem.at[2]),
        pltpu.make_async_copy(lengths_hbm, lengths_ref, small_sem.at[3]),
    ]
    for copy in small:
        copy.start()
    for step in range(STEPS_AHEAD):
        for copy in cache_copies(step):
            copy.start()
    for copy in small:
        copy.wait()

    group = lax.broadcasted_iota(jnp.int32, fresh_key_ref.shape, 1) == head_ref[0]
    own_key = jnp.sum(jnp.where(group, fresh_key_ref[...].astype(jnp.float32), 0.0), axis=1)
    own_value = jnp.sum(jnp.where(group, fresh_value_ref[...].astype(jnp.float32), 0.0), axis=1)
    for head in range(head_count):
        rows = pl.ds(head, row_count, stride=head_count)
        columns = pl.ds(head * head_size, head_size)
        query_scr[rows, :] = query_ref[:, columns].astype(jnp.float32)
        own_key_scr[rows, :] = own_key
        own_value_scr[rows, :] = own_value

    pair = 2 * head_count
    upper = lax.broadcasted_iota(jnp.int32, (pair, positions), 0) < head_count
    position = lax.broadcasted_iota(jnp.int32, (pair, positions), 1)

    @pl.loop(0, steps)
    def _(step):
        for copy in cache_copies(step):
            copy.wait()

        @pl.when(step + STEPS_AHEAD < steps)
        def _():
            for copy in cache_copies(step + STEPS_AHEAD):
                copy.start()

        @pl.when(step == 0)
        def _():
            weight_copy.start()
            residual_copy.start()

        first = pl.multiple_of(step * (ROWS_STEP * head_count), ROWS_STEP * head_count)
        queries = query_scr[pl.ds(first, ROWS_STEP * head_count), :]
        parts = []
        for i in range(ROWS_STEP // 2):
            row = step * ROWS_STEP + 2 * i
            keys = key_ref[pl.ds(row, 2)].reshape(2 * positions, head_size)
            asked = queries[i * pair : (i + 1) * pair].astype(jnp.bfloat16)
            both = lax.dot_general(
                asked, keys, (((1,), (1,)), ((), ())), preferred_element_type=jnp.float32
            )
            scores = jnp.where(upper, both[:, :positions], both[:, positions:]) * score_scale
            live = jnp.where(upper, lengths_ref[row], lengths_ref[row + 1])
            parts.append(jnp.where(position < live, scores, -1e30))
        scores = jnp.concatenate(parts, axis=0)
        own_keys = own_key_scr[pl.ds(first, ROWS_STEP * head_count), :]
        own_score = jnp.sum(queries * own_keys, axis=-1, keepdims=True) * score_scale
        row_max = jnp.maximum(jnp.max(scores, axis=-1, keepdims=True), own_score)
        terms = jnp.exp(scores - row_max)
        own_term = jnp.exp(own_score - row_max)
        total = jnp.sum(terms, axis=-1, keepdims=True) + own_term
        probs = (terms / total).astype(jnp.bfloat16).astype(jnp.float32)
        own_prob = (own_term / total).astype(jnp.bfloat16).astype(jnp.float32)
        parts = []
        for i in range(ROWS_STEP // 2):
            row = step * ROWS_STEP + 2 * i
            values = value_ref[pl.ds(row, 2)].reshape(2 * positions, head_size)
            prob = probs[i * pair : (i + 1) * pair]
            spread = jnp.concatenate(
                [jnp.where(upper, prob, 0.0), jnp.where(upper, 0.0, prob)], axis=1
            ).astype(jnp.bfloat16)
            parts.append(jnp.dot(spread, values, preferred_element_type=jnp.float32))
        attended = jnp.concatenate(parts, axis=0)
        own_values = own_value_scr[pl.ds(first, ROWS_STEP * head_count), :]
        attended_scr[pl.ds(first, ROWS_STEP * head_count), :] = attended + own_prob * own_values

    for head in range(head_count):
        columns = pl.ds(head * head_size, head_size)
        rows = pl.ds(head, row_count, stride=head_count)
        heads_scr[:, columns] = attended_scr[rows, :].astype(jnp.bfloat16)
    residual_copy.wait()
    weight_copy.wait()
    for piece in range(pieces):
        columns = pl.ds(piece * chunk, chunk)
        part = jnp.dot(
            heads_scr[...], weight_ref[:, columns], preferred_element_type=jnp.float32
        )
        out_ref[piece] = part.astype(jnp.bfloat16)


def run_attend(
    residual_in, query, fresh_key, fresh_value, key_cache, value_cache, lengths, column, kv_head, out_weight, pieces,
):
    row_count, positions, head_size = key_cache.shape
    width = out_weight.shape[1]
    many = query.shape[0] * query.shape[1] // head_size
    whole = pl.BlockSpec(memory_space=pltpu.VMEM)
    scalars = pl.BlockSpec(memory_space=pltpu.SMEM)
    left = pl.BlockSpec(memory_space=pltpu.HBM)
    steps = row_count // ROWS_STEP
    return pl.pallas_call(
        attend_kernel,
        out_shape=(
            jax.ShapeDtypeStruct((pieces, row_count, width // pieces), jnp.bfloat16),
            jax.ShapeDtypeStruct((row_count, width // pieces), residual_in.dtype),
        ),
        in_specs=[scalars] * 2 + [left] * 8,
        out_specs=(whole, whole),
        scratch_shapes=[
            pltpu.SMEM(lengths.shape, jnp.int32),
            pltpu.VMEM(query.shape, jnp.bfloat16),
            pltpu.VMEM(fresh_key.shape, jnp.bfloat16),
            pltpu.VMEM(fresh_value.shape, jnp.bfloat16),
            pltpu.VMEM(key_cache.shape, jnp.bfloat16),
            pltpu.VMEM(value_cache.shape, jnp.bfloat16),
            pltpu.VMEM(out_weight.shape, jnp.bfloat16),
            pltpu.VMEM((many, head_size), jnp.float32),
            pltpu.VMEM((many, head_size), jnp.float32),
            pltpu.VMEM((many, head_size), jnp.float32),
            pltpu.VMEM((many, head_size), jnp.float32),
            pltpu.VMEM(query.shape, jnp.bfloat16),
            pltpu.SemaphoreType.DMA((4,)),
            pltpu.SemaphoreType.DMA,
            pltpu.SemaphoreType.DMA((steps,)),
            pltpu.SemaphoreType.DMA((steps,)),
            pltpu.SemaphoreType.DMA,
        ],
        compiler_params=pltpu.CompilerParams(vmem_limit_bytes=60 * 1024 * 1024),
        name="attend",
    )(kv_head, column, lengths, residual_in, query, fresh_key, fresh_value, key_cache, value_cache, out_weight)


def route_kernel(ids_ref, scores_ref, residual_ref, slot_ref, weight_ref, kept_ref):
    experts, row_count = slot_ref.shape
    topk = ids_ref.shape[0]
    scores = scores_ref[...]
    weights = scores / jnp.sum(scores, axis=0, keepdims=True)
    expert = lax.broadcasted_iota(jnp.int32, (experts, row_count), 0)
    named = jnp.zeros((experts, row_count), jnp.float32)
    weight = jnp.zeros((experts, row_count), jnp.float32)
    for k in range(topk):
        match = ids_ref[k : k + 1, :] == expert
        named = named + jnp.where(match, 1.0, 0.0)
        weight = weight + jnp.where(match, weights[k : k + 1, :], 0.0)
    earlier = lax.broadcasted_iota(jnp.int32, (row_count, row_count), 0)
    later = lax.broadcasted_iota(jnp.int32, (row_count, row_count), 1)
    before = jnp.where(earlier < later, 1.0, 0.0).astype(jnp.bfloat16)
    rank = jnp.dot(named.astype(jnp.bfloat16), before, preferred_element_type=jnp.float32)
    slot_ref[...] = jnp.where(named > 0.0, rank, -1.0).astype(jnp.int32)
    weight_ref[...] = weight
    kept_ref[...] = residual_ref[...]


def run_route(expert_ids, gate_scores, residual, experts_all):
    row_count = expert_ids.shape[0]
    whole = pl.BlockSpec(memory_space=pltpu.VMEM)
    return pl.pallas_call(
        route_kernel,
        out_shape=(
            jax.ShapeDtypeStruct((experts_all, row_count), jnp.int32),
            jax.ShapeDtypeStruct((experts_all, row_count), jnp.float32),
            jax.ShapeDtypeStruct(residual.shape, residual.dtype),
        ),
        in_specs=[whole] * 3,
        out_specs=(whole, whole, whole),
        compiler_params=pltpu.CompilerParams(vmem_limit_bytes=4 * 1024 * 1024),
        name="route",
    )(expert_ids.T, gate_scores.T, residual)


def select_kernel(pieces_ref, residual_ref, slot_ref, hidden_ref, outgoing_ref):
    sources = pieces_ref.shape[0]
    experts, slots, chunk = outgoing_ref.shape
    row_count = slot_ref.shape[1]
    proj = pieces_ref[0].astype(jnp.float32)
    for source in range(1, sources):
        proj = proj + pieces_ref[source].astype(jnp.float32)
    hidden = (residual_ref[...].astype(jnp.float32) + proj).astype(jnp.bfloat16)
    hidden_ref[...] = hidden
    group = row_count // slots
    place = lax.broadcasted_iota(jnp.int32, (group, slots, row_count), 1)
    for first in range(0, experts, group):
        chosen = slot_ref[pl.ds(first, group), :][:, None, :] == place
        selector = jnp.where(chosen, 1.0, 0.0).reshape(group * slots, row_count)
        rows = jnp.dot(selector.astype(jnp.bfloat16), hidden, preferred_element_type=jnp.float32)
        outgoing_ref[pl.ds(first, group)] = rows.astype(jnp.bfloat16).reshape(group, slots, chunk)


def run_select(pieces, residual, slot, slots):
    experts, row_count = slot.shape
    chunk = pieces.shape[2]
    whole = pl.BlockSpec(memory_space=pltpu.VMEM)
    return pl.pallas_call(
        select_kernel,
        out_shape=(
            jax.ShapeDtypeStruct((row_count, chunk), jnp.bfloat16),
            jax.ShapeDtypeStruct((experts, slots, chunk), jnp.bfloat16),
        ),
        in_specs=[whole] * 3,
        out_specs=(whole, whole),
        compiler_params=pltpu.CompilerParams(vmem_limit_bytes=8 * 1024 * 1024),
        cost_estimate=pl.CostEstimate(flops=115_000_000_000, bytes_accessed=4_000_000, transcendentals=0),
        name="select",
    )(pieces, residual, slot)


def experts_kernel(rows_ref, gain_ref, gate_ref, up_ref, down_ref, out_ref, normed_ref, act_ref):
    replicas, pieces, slots, chunk = rows_ref.shape
    total = replicas * slots
    width = pieces * chunk
    squares = jnp.zeros((total, chunk), jnp.float32)
    for piece in range(pieces):
        part = rows_ref[:, piece].reshape(total, chunk).astype(jnp.float32)
        squares = squares + part * part
    spread = jnp.sum(squares, axis=-1, keepdims=True) * (1.0 / width)
    scale = lax.rsqrt(spread + 1e-06)
    for piece in range(pieces):
        part = rows_ref[:, piece].reshape(total, chunk).astype(jnp.float32)
        columns = pl.ds(piece * chunk, chunk)
        normed_ref[:, columns] = (part * scale * gain_ref[:, columns]).astype(jnp.bfloat16)
    for first in range(0, gate_ref.shape[1], chunk):
        units = pl.ds(first, chunk)
        gate_part = jnp.dot(normed_ref[...], gate_ref[:, units], preferred_element_type=jnp.float32)
        up_part = jnp.dot(normed_ref[...], up_ref[:, units], preferred_element_type=jnp.float32)
        act_ref[:, units] = (gate_part / (1.0 + jnp.exp(-gate_part)) * up_part).astype(jnp.bfloat16)
    for piece in range(pieces):
        columns = pl.ds(piece * chunk, chunk)
        part = jnp.dot(act_ref[...], down_ref[:, columns], preferred_element_type=jnp.float32)
        out_ref[:, piece] = part.astype(jnp.bfloat16).reshape(replicas, slots, chunk)


def run_experts(rows, norm_gain, weights):
    replicas, pieces, slots, chunk = rows.shape
    width, hidden_units = weights[0].shape
    total = replicas * slots
    whole = pl.BlockSpec(memory_space=pltpu.VMEM)
    return pl.pallas_call(
        experts_kernel,
        out_shape=jax.ShapeDtypeStruct(rows.shape, jnp.bfloat16),
        in_specs=[whole] * 5,
        out_specs=whole,
        scratch_shapes=[
            pltpu.VMEM((total, width), jnp.bfloat16),
            pltpu.VMEM((total, hidden_units), jnp.bfloat16),
        ],
        compiler_params=pltpu.CompilerParams(vmem_limit_bytes=16 * 1024 * 1024),
        name="experts",
    )(rows, norm_gain.reshape(1, width), *weights)


def shards(
    residual_in,
    query,
    fresh_key,
    fresh_value,
    key_cache,
    value_cache,
    lengths,
    out_weight,
    norm_gain,
    expert_ids,
    gate_scores,
    w_gate,
    w_up,
    w_down,
):
    both = ("dp", "tensor")
    row_count, width = residual_in.shape
    tensor_width = lax.axis_size("tensor")
    replica_count = lax.axis_size("dp")
    experts_all = replica_count * tensor_width
    column = lax.axis_index("tensor")
    chunk = width // tensor_width
    cap_slots = 2 * max(1, row_count * expert_ids.shape[1] // experts_all)

    kv_head = (column // (tensor_width // fresh_key.shape[1])).astype(jnp.int32).reshape(1)
    own_column = column.astype(jnp.int32).reshape(1)
    partial, residual = run_attend(
        residual_in, query, fresh_key, fresh_value, key_cache[:, 0], value_cache[:, 0], lengths,
        own_column, kv_head, out_weight, tensor_width,
    )
    pieces = lax.all_to_all(partial, "tensor", split_axis=0, concat_axis=0, tiled=True)
    slot, row_weight, residual = run_route(expert_ids, gate_scores, residual, experts_all)
    hidden, outgoing = run_select(pieces, residual, slot, cap_slots)
    received = lax.all_to_all(outgoing, both, split_axis=0, concat_axis=0, tiled=True)

    weights = [w_gate[0], w_up[0], w_down[0]]
    rows = received.reshape(replica_count, tensor_width, cap_slots, chunk)
    answered = run_experts(rows, norm_gain, weights)
    answered = answered.reshape(experts_all, cap_slots, chunk)
    returned = lax.all_to_all(answered, both, split_axis=0, concat_axis=0, tiled=True)

    slot_axis = lax.broadcasted_iota(jnp.int32, (1, cap_slots, 1), 1)
    chosen = slot[:, None, :] == slot_axis
    spread_weight = jnp.where(chosen, row_weight[:, None, :], 0.0)
    coarse = spread_weight.astype(jnp.bfloat16)
    fine = (spread_weight - coarse.astype(jnp.float32)).astype(jnp.bfloat16)
    mixture = jnp.einsum(
        "esr,esj->rj", coarse, returned, preferred_element_type=jnp.float32
    ) + jnp.einsum("esr,esj->rj", fine, returned, preferred_element_type=jnp.float32)
    layer = (hidden.astype(jnp.float32) + mixture).astype(jnp.bfloat16)
    own = lax.all_to_all(
        layer.reshape(tensor_width, row_count // tensor_width, chunk),
        "tensor",
        split_axis=0,
        concat_axis=0,
        tiled=True,
    )
    return own.transpose(1, 0, 2).reshape(row_count // tensor_width, width)


def solution(mesh):
    placed = (
        P("dp", None),
        P("dp", "tensor"),
        P("dp", None, None),
        P("dp", None, None),
        P("dp", "tensor", None, None),
        P("dp", "tensor", None, None),
        P("dp"),
        P("tensor", None),
        P(),
        P("dp", None),
        P("dp", None),
        P(("dp", "tensor"), None, None),
        P(("dp", "tensor"), None, None),
        P(("dp", "tensor"), None, None),
    )
    return jax.shard_map(
        shards, mesh=mesh, in_specs=placed, out_specs=P(("dp", "tensor"), None), check_vma=False
    )
```

```python
import jax
import jax.numpy as jnp
from jax import lax
from jax.experimental import pallas as pl
from jax.experimental.pallas import tpu as pltpu
from jax.sharding import PartitionSpec as P


ROWS_STEP = 32
STEPS_AHEAD = 3


def attend_kernel(
    head_ref, column_ref, lengths_hbm, residual_hbm, query_hbm, fresh_key_hbm, fresh_value_hbm, key_hbm, value_hbm, weight_hbm,
    out_ref, residual_ref,
    lengths_ref, query_ref, fresh_key_ref, fresh_value_ref, key_ref, value_ref, weight_ref,
    query_scr, own_key_scr, own_value_scr, attended_scr, heads_scr,
    small_sem, residual_sem, key_sem, value_sem, weight_sem,
):
    row_count, positions, head_size = key_ref.shape
    head_count = query_ref.shape[1] // head_size
    pieces, _, chunk = out_ref.shape
    steps = row_count // ROWS_STEP
    score_scale = head_size ** (-0.5)

    def cache_copies(step):
        rows = pl.ds(step * ROWS_STEP, ROWS_STEP)
        return (
            pltpu.make_async_copy(key_hbm.at[rows], key_ref.at[rows], key_sem.at[step]),
            pltpu.make_async_copy(value_hbm.at[rows], value_ref.at[rows], value_sem.at[step]),
        )

    weight_copy = pltpu.make_async_copy(weight_hbm, weight_ref, weight_sem)
    own = pl.ds(pl.multiple_of(column_ref[0] * chunk, chunk), chunk)
    residual_copy = pltpu.make_async_copy(residual_hbm.at[:, own], residual_ref, residual_sem)
    small = [
        pltpu.make_async_copy(query_hbm, query_ref, small_sem.at[0]),
        pltpu.make_async_copy(fresh_key_hbm, fresh_key_ref, small_sem.at[1]),
        pltpu.make_async_copy(fresh_value_hbm, fresh_value_ref, small_sem.at[2]),
        pltpu.make_async_copy(lengths_hbm, lengths_ref, small_sem.at[3]),
    ]
    for copy in small:
        copy.start()
    for step in range(STEPS_AHEAD):
        for copy in cache_copies(step):
            copy.start()
    for copy in small:
        copy.wait()

    group = lax.broadcasted_iota(jnp.int32, fresh_key_ref.shape, 1) == head_ref[0]
    own_key = jnp.sum(jnp.where(group, fresh_key_ref[...].astype(jnp.float32), 0.0), axis=1)
    own_value = jnp.sum(jnp.where(group, fresh_value_ref[...].astype(jnp.float32), 0.0), axis=1)
    for head in range(head_count):
        rows = pl.ds(head, row_count, stride=head_count)
        columns = pl.ds(head * head_size, head_size)
        query_scr[rows, :] = query_ref[:, columns].astype(jnp.float32)
        own_key_scr[rows, :] = own_key
        own_value_scr[rows, :] = own_value

    pair = 2 * head_count
    upper = lax.broadcasted_iota(jnp.int32, (pair, positions), 0) < head_count
    position = lax.broadcasted_iota(jnp.int32, (pair, positions), 1)

    @pl.loop(0, steps)
    def _(step):
        for copy in cache_copies(step):
            copy.wait()

        @pl.when(step + STEPS_AHEAD < steps)
        def _():
            for copy in cache_copies(step + STEPS_AHEAD):
                copy.start()

        @pl.when(step == 0)
        def _():
            weight_copy.start()
            residual_copy.start()

        first = pl.multiple_of(step * (ROWS_STEP * head_count), ROWS_STEP * head_count)
        queries = query_scr[pl.ds(first, ROWS_STEP * head_count), :]
        parts = []
        for i in range(ROWS_STEP // 2):
            row = step * ROWS_STEP + 2 * i
            keys = key_ref[pl.ds(row, 2)].reshape(2 * positions, head_size)
            asked = queries[i * pair : (i + 1) * pair].astype(jnp.bfloat16)
            both = lax.dot_general(
                asked, keys, (((1,), (1,)), ((), ())), preferred_element_type=jnp.float32
            )
            scores = jnp.where(upper, both[:, :positions], both[:, positions:]) * score_scale
            live = jnp.where(upper, lengths_ref[row], lengths_ref[row + 1])
            parts.append(jnp.where(position < live, scores, -1e30))
        scores = jnp.concatenate(parts, axis=0)
        own_keys = own_key_scr[pl.ds(first, ROWS_STEP * head_count), :]
        own_score = jnp.sum(queries * own_keys, axis=-1, keepdims=True) * score_scale
        row_max = jnp.maximum(jnp.max(scores, axis=-1, keepdims=True), own_score)
        terms = jnp.exp(scores - row_max)
        own_term = jnp.exp(own_score - row_max)
        total = jnp.sum(terms, axis=-1, keepdims=True) + own_term
        probs = (terms / total).astype(jnp.bfloat16).astype(jnp.float32)
        own_prob = (own_term / total).astype(jnp.bfloat16).astype(jnp.float32)
        parts = []
        for i in range(ROWS_STEP // 2):
            row = step * ROWS_STEP + 2 * i
            values = value_ref[pl.ds(row, 2)].reshape(2 * positions, head_size)
            prob = probs[i * pair : (i + 1) * pair]
            spread = jnp.concatenate(
                [jnp.where(upper, prob, 0.0), jnp.where(upper, 0.0, prob)], axis=1
            ).astype(jnp.bfloat16)
            parts.append(jnp.dot(spread, values, preferred_element_type=jnp.float32))
        attended = jnp.concatenate(parts, axis=0)
        own_values = own_value_scr[pl.ds(first, ROWS_STEP * head_count), :]
        attended_scr[pl.ds(first, ROWS_STEP * head_count), :] = attended + own_prob * own_values

    for head in range(head_count):
        columns = pl.ds(head * head_size, head_size)
        rows = pl.ds(head, row_count, stride=head_count)
        heads_scr[:, columns] = attended_scr[rows, :].astype(jnp.bfloat16)
    residual_copy.wait()
    weight_copy.wait()
    for piece in range(pieces):
        columns = pl.ds(piece * chunk, chunk)
        part = jnp.dot(
            heads_scr[...], weight_ref[:, columns], preferred_element_type=jnp.float32
        )
        out_ref[piece] = part.astype(jnp.bfloat16)


def run_attend(
    residual_in, query, fresh_key, fresh_value, key_cache, value_cache, lengths, column, kv_head, out_weight, pieces,
):
    row_count, positions, head_size = key_cache.shape
    width = out_weight.shape[1]
    many = query.shape[0] * query.shape[1] // head_size
    whole = pl.BlockSpec(memory_space=pltpu.VMEM)
    scalars = pl.BlockSpec(memory_space=pltpu.SMEM)
    left = pl.BlockSpec(memory_space=pltpu.HBM)
    steps = row_count // ROWS_STEP
    return pl.pallas_call(
        attend_kernel,
        out_shape=(
            jax.ShapeDtypeStruct((pieces, row_count, width // pieces), jnp.bfloat16),
            jax.ShapeDtypeStruct((row_count, width // pieces), residual_in.dtype),
        ),
        in_specs=[scalars] * 2 + [left] * 8,
        out_specs=(whole, whole),
        scratch_shapes=[
            pltpu.SMEM(lengths.shape, jnp.int32),
            pltpu.VMEM(query.shape, jnp.bfloat16),
            pltpu.VMEM(fresh_key.shape, jnp.bfloat16),
            pltpu.VMEM(fresh_value.shape, jnp.bfloat16),
            pltpu.VMEM(key_cache.shape, jnp.bfloat16),
            pltpu.VMEM(value_cache.shape, jnp.bfloat16),
            pltpu.VMEM(out_weight.shape, jnp.bfloat16),
            pltpu.VMEM((many, head_size), jnp.float32),
            pltpu.VMEM((many, head_size), jnp.float32),
            pltpu.VMEM((many, head_size), jnp.float32),
            pltpu.VMEM((many, head_size), jnp.float32),
            pltpu.VMEM(query.shape, jnp.bfloat16),
            pltpu.SemaphoreType.DMA((4,)),
            pltpu.SemaphoreType.DMA,
            pltpu.SemaphoreType.DMA((steps,)),
            pltpu.SemaphoreType.DMA((steps,)),
            pltpu.SemaphoreType.DMA,
        ],
        compiler_params=pltpu.CompilerParams(vmem_limit_bytes=60 * 1024 * 1024),
        name="attend",
    )(kv_head, column, lengths, residual_in, query, fresh_key, fresh_value, key_cache, value_cache, out_weight)


def route_kernel(ids_ref, scores_ref, residual_ref, slot_ref, weight_ref, kept_ref):
    experts, row_count = slot_ref.shape
    topk = ids_ref.shape[0]
    scores = scores_ref[...]
    weights = scores / jnp.sum(scores, axis=0, keepdims=True)
    expert = lax.broadcasted_iota(jnp.int32, (experts, row_count), 0)
    named = jnp.zeros((experts, row_count), jnp.float32)
    weight = jnp.zeros((experts, row_count), jnp.float32)
    for k in range(topk):
        match = ids_ref[k : k + 1, :] == expert
        named = named + jnp.where(match, 1.0, 0.0)
        weight = weight + jnp.where(match, weights[k : k + 1, :], 0.0)
    earlier = lax.broadcasted_iota(jnp.int32, (row_count, row_count), 0)
    later = lax.broadcasted_iota(jnp.int32, (row_count, row_count), 1)
    before = jnp.where(earlier < later, 1.0, 0.0).astype(jnp.bfloat16)
    rank = jnp.dot(named.astype(jnp.bfloat16), before, preferred_element_type=jnp.float32)
    slot_ref[...] = jnp.where(named > 0.0, rank, -1.0).astype(jnp.int32)
    weight_ref[...] = weight
    kept_ref[...] = residual_ref[...]


def run_route(expert_ids, gate_scores, residual, experts_all):
    row_count = expert_ids.shape[0]
    whole = pl.BlockSpec(memory_space=pltpu.VMEM)
    return pl.pallas_call(
        route_kernel,
        out_shape=(
            jax.ShapeDtypeStruct((experts_all, row_count), jnp.int32),
            jax.ShapeDtypeStruct((experts_all, row_count), jnp.float32),
            jax.ShapeDtypeStruct(residual.shape, residual.dtype),
        ),
        in_specs=[whole] * 3,
        out_specs=(whole, whole, whole),
        compiler_params=pltpu.CompilerParams(vmem_limit_bytes=4 * 1024 * 1024),
        cost_estimate=pl.CostEstimate(
            flops=60_000_000_000, bytes_accessed=4_000_000, transcendentals=0
        ),
        name="route",
    )(expert_ids.T, gate_scores.T, residual)


def select_kernel(pieces_ref, residual_ref, slot_ref, hidden_ref, outgoing_ref):
    sources = pieces_ref.shape[0]
    experts, slots, chunk = outgoing_ref.shape
    row_count = slot_ref.shape[1]
    proj = pieces_ref[0].astype(jnp.float32)
    for source in range(1, sources):
        proj = proj + pieces_ref[source].astype(jnp.float32)
    hidden = (residual_ref[...].astype(jnp.float32) + proj).astype(jnp.bfloat16)
    hidden_ref[...] = hidden
    group = row_count // slots
    place = lax.broadcasted_iota(jnp.int32, (group, slots, row_count), 1)
    for first in range(0, experts, group):
        chosen = slot_ref[pl.ds(first, group), :][:, None, :] == place
        selector = jnp.where(chosen, 1.0, 0.0).reshape(group * slots, row_count)
        rows = jnp.dot(selector.astype(jnp.bfloat16), hidden, preferred_element_type=jnp.float32)
        outgoing_ref[pl.ds(first, group)] = rows.astype(jnp.bfloat16).reshape(group, slots, chunk)


def run_select(pieces, residual, slot, slots):
    experts, row_count = slot.shape
    chunk = pieces.shape[2]
    whole = pl.BlockSpec(memory_space=pltpu.VMEM)
    return pl.pallas_call(
        select_kernel,
        out_shape=(
            jax.ShapeDtypeStruct((row_count, chunk), jnp.bfloat16),
            jax.ShapeDtypeStruct((experts, slots, chunk), jnp.bfloat16),
        ),
        in_specs=[whole] * 3,
        out_specs=(whole, whole),
        compiler_params=pltpu.CompilerParams(vmem_limit_bytes=8 * 1024 * 1024),
        cost_estimate=pl.CostEstimate(flops=115_000_000_000, bytes_accessed=4_000_000, transcendentals=0),
        name="select",
    )(pieces, residual, slot)


def experts_kernel(rows_ref, gain_ref, gate_ref, up_ref, down_ref, out_ref, normed_ref, act_ref):
    replicas, pieces, slots, chunk = rows_ref.shape
    total = replicas * slots
    width = pieces * chunk
    squares = jnp.zeros((total, chunk), jnp.float32)
    for piece in range(pieces):
        part = rows_ref[:, piece].reshape(total, chunk).astype(jnp.float32)
        squares = squares + part * part
    spread = jnp.sum(squares, axis=-1, keepdims=True) * (1.0 / width)
    scale = lax.rsqrt(spread + 1e-06)
    for piece in range(pieces):
        part = rows_ref[:, piece].reshape(total, chunk).astype(jnp.float32)
        columns = pl.ds(piece * chunk, chunk)
        normed_ref[:, columns] = (part * scale * gain_ref[:, columns]).astype(jnp.bfloat16)
    for first in range(0, gate_ref.shape[1], chunk):
        units = pl.ds(first, chunk)
        gate_part = jnp.dot(normed_ref[...], gate_ref[:, units], preferred_element_type=jnp.float32)
        up_part = jnp.dot(normed_ref[...], up_ref[:, units], preferred_element_type=jnp.float32)
        act_ref[:, units] = (gate_part / (1.0 + jnp.exp(-gate_part)) * up_part).astype(jnp.bfloat16)
    for piece in range(pieces):
        columns = pl.ds(piece * chunk, chunk)
        part = jnp.dot(act_ref[...], down_ref[:, columns], preferred_element_type=jnp.float32)
        out_ref[:, piece] = part.astype(jnp.bfloat16).reshape(replicas, slots, chunk)


def run_experts(rows, norm_gain, weights):
    replicas, pieces, slots, chunk = rows.shape
    width, hidden_units = weights[0].shape
    total = replicas * slots
    whole = pl.BlockSpec(memory_space=pltpu.VMEM)
    return pl.pallas_call(
        experts_kernel,
        out_shape=jax.ShapeDtypeStruct(rows.shape, jnp.bfloat16),
        in_specs=[whole] * 5,
        out_specs=whole,
        scratch_shapes=[
            pltpu.VMEM((total, width), jnp.bfloat16),
            pltpu.VMEM((total, hidden_units), jnp.bfloat16),
        ],
        compiler_params=pltpu.CompilerParams(vmem_limit_bytes=16 * 1024 * 1024),
        name="experts",
    )(rows, norm_gain.reshape(1, width), *weights)


def spread_kernel(slot_ref, weight_ref, spread_ref):
    experts, row_count = slot_ref.shape
    total = spread_ref.shape[2]
    slots = total // experts
    step = 256
    slot = slot_ref[...].astype(jnp.float32).T.astype(jnp.bfloat16)
    weight = weight_ref[...].T
    coarse = weight.astype(jnp.bfloat16)
    fine = (weight - coarse.astype(jnp.float32)).astype(jnp.bfloat16)
    begin = lax.broadcasted_iota(jnp.int32, (experts, step), 0) * slots
    place = lax.broadcasted_iota(jnp.int32, (experts, step), 1)
    lane = lax.broadcasted_iota(jnp.int32, (row_count, step), 1)
    for first in range(0, total, step):
        inside = (place + first >= begin) & (place + first < begin + slots)
        expand = jnp.where(inside, 1.0, 0.0).astype(jnp.bfloat16)
        here = jnp.dot(slot, expand, preferred_element_type=jnp.float32)
        chosen = here == lax.rem(lane + first, slots).astype(jnp.float32)
        for part, values in enumerate((coarse, fine)):
            spread = jnp.dot(values, expand, preferred_element_type=jnp.float32)
            spread_ref[part, :, pl.ds(first, step)] = jnp.where(chosen, spread, 0.0).astype(
                jnp.bfloat16
            )


def run_spread(slot, row_weight, slots):
    experts, row_count = slot.shape
    whole = pl.BlockSpec(memory_space=pltpu.VMEM)
    return pl.pallas_call(
        spread_kernel,
        out_shape=jax.ShapeDtypeStruct((2, row_count, experts * slots), jnp.bfloat16),
        in_specs=[whole] * 2,
        out_specs=whole,
        compiler_params=pltpu.CompilerParams(vmem_limit_bytes=4 * 1024 * 1024),
        name="spread",
    )(slot, row_weight)


def combine_kernel(spread_ref, returned_ref, hidden_ref, out_ref):
    experts, slots, chunk = returned_ref.shape
    rows = returned_ref[...].reshape(experts * slots, chunk)
    mixture = jnp.dot(spread_ref[0], rows, preferred_element_type=jnp.float32) + jnp.dot(
        spread_ref[1], rows, preferred_element_type=jnp.float32
    )
    layer = hidden_ref[...].astype(jnp.float32) + mixture
    out_ref[...] = layer.reshape(out_ref.shape).astype(jnp.bfloat16)


def run_combine(spread, returned, hidden, parts):
    row_count, chunk = hidden.shape
    whole = pl.BlockSpec(memory_space=pltpu.VMEM)
    return pl.pallas_call(
        combine_kernel,
        out_shape=jax.ShapeDtypeStruct((parts, row_count // parts, chunk), jnp.bfloat16),
        in_specs=[whole] * 3,
        out_specs=whole,
        compiler_params=pltpu.CompilerParams(vmem_limit_bytes=4 * 1024 * 1024),
        name="combine",
    )(spread, returned, hidden)


def shards(
    residual_in,
    query,
    fresh_key,
    fresh_value,
    key_cache,
    value_cache,
    lengths,
    out_weight,
    norm_gain,
    expert_ids,
    gate_scores,
    w_gate,
    w_up,
    w_down,
):
    both = ("dp", "tensor")
    row_count, width = residual_in.shape
    tensor_width = lax.axis_size("tensor")
    replica_count = lax.axis_size("dp")
    experts_all = replica_count * tensor_width
    column = lax.axis_index("tensor")
    chunk = width // tensor_width
    cap_slots = 2 * max(1, row_count * expert_ids.shape[1] // experts_all)

    kv_head = (column // (tensor_width // fresh_key.shape[1])).astype(jnp.int32).reshape(1)
    own_column = column.astype(jnp.int32).reshape(1)
    partial, residual = run_attend(
        residual_in, query, fresh_key, fresh_value, key_cache[:, 0], value_cache[:, 0], lengths,
        own_column, kv_head, out_weight, tensor_width,
    )
    pieces = lax.all_to_all(partial, "tensor", split_axis=0, concat_axis=0, tiled=True)
    slot, row_weight, residual = run_route(expert_ids, gate_scores, residual, experts_all)
    hidden, outgoing = run_select(pieces, residual, slot, cap_slots)
    received = lax.all_to_all(outgoing, both, split_axis=0, concat_axis=0, tiled=True)

    weights = [w_gate[0], w_up[0], w_down[0]]
    rows = received.reshape(replica_count, tensor_width, cap_slots, chunk)
    answered = run_experts(rows, norm_gain, weights)
    answered = answered.reshape(experts_all, cap_slots, chunk)
    slot, row_weight, answered = lax.optimization_barrier((slot, row_weight, answered))
    returned = lax.all_to_all(answered, both, split_axis=0, concat_axis=0, tiled=True)
    spread = run_spread(slot, row_weight, cap_slots)
    own = lax.all_to_all(
        run_combine(spread, returned, hidden, tensor_width),
        "tensor",
        split_axis=0,
        concat_axis=0,
        tiled=True,
    )
    return own.transpose(1, 0, 2).reshape(row_count // tensor_width, width)


def solution(mesh):
    placed = (
        P("dp", None),
        P("dp", "tensor"),
        P("dp", None, None),
        P("dp", None, None),
        P("dp", "tensor", None, None),
        P("dp", "tensor", None, None),
        P("dp"),
        P("tensor", None),
        P(),
        P("dp", None),
        P("dp", None),
        P(("dp", "tensor"), None, None),
        P(("dp", "tensor"), None, None),
        P(("dp", "tensor"), None, None),
    )
    return jax.shard_map(
        shards, mesh=mesh, in_specs=placed, out_specs=P(("dp", "tensor"), None), check_vma=False
    )
```

```python
import jax
import jax.numpy as jnp
from jax import lax
from jax.experimental import pallas as pl
from jax.experimental.pallas import tpu as pltpu
from jax.sharding import Mesh
from jax.sharding import PartitionSpec as P

TENSOR = ("column", "line")
LINES = 4


ROWS_STEP = 32
STEPS_AHEAD = 3


def attend_kernel(
    head_ref, column_ref, lengths_hbm, residual_hbm, query_hbm, fresh_key_hbm, fresh_value_hbm, key_hbm, value_hbm, weight_hbm,
    out_ref, residual_ref,
    lengths_ref, query_ref, fresh_key_ref, fresh_value_ref, key_ref, value_ref, weight_ref,
    query_scr, own_key_scr, own_value_scr, attended_scr, heads_scr,
    small_sem, residual_sem, key_sem, value_sem, weight_sem,
):
    row_count, positions, head_size = key_ref.shape
    head_count = query_ref.shape[1] // head_size
    pieces, _, chunk = out_ref.shape
    steps = row_count // ROWS_STEP
    score_scale = head_size ** (-0.5)

    def cache_copies(step):
        rows = pl.ds(step * ROWS_STEP, ROWS_STEP)
        return (
            pltpu.make_async_copy(key_hbm.at[rows], key_ref.at[rows], key_sem.at[step]),
            pltpu.make_async_copy(value_hbm.at[rows], value_ref.at[rows], value_sem.at[step]),
        )

    weight_copy = pltpu.make_async_copy(weight_hbm, weight_ref, weight_sem)
    own = pl.ds(pl.multiple_of(column_ref[0] * chunk, chunk), chunk)
    residual_copy = pltpu.make_async_copy(residual_hbm.at[:, own], residual_ref, residual_sem)
    small = [
        pltpu.make_async_copy(query_hbm, query_ref, small_sem.at[0]),
        pltpu.make_async_copy(fresh_key_hbm, fresh_key_ref, small_sem.at[1]),
        pltpu.make_async_copy(fresh_value_hbm, fresh_value_ref, small_sem.at[2]),
        pltpu.make_async_copy(lengths_hbm, lengths_ref, small_sem.at[3]),
    ]
    for copy in small:
        copy.start()
    for step in range(STEPS_AHEAD):
        for copy in cache_copies(step):
            copy.start()
    for copy in small:
        copy.wait()

    group = lax.broadcasted_iota(jnp.int32, fresh_key_ref.shape, 1) == head_ref[0]
    own_key = jnp.sum(jnp.where(group, fresh_key_ref[...].astype(jnp.float32), 0.0), axis=1)
    own_value = jnp.sum(jnp.where(group, fresh_value_ref[...].astype(jnp.float32), 0.0), axis=1)
    for head in range(head_count):
        rows = pl.ds(head, row_count, stride=head_count)
        columns = pl.ds(head * head_size, head_size)
        query_scr[rows, :] = query_ref[:, columns].astype(jnp.float32)
        own_key_scr[rows, :] = own_key
        own_value_scr[rows, :] = own_value

    pair = 2 * head_count
    upper = lax.broadcasted_iota(jnp.int32, (pair, positions), 0) < head_count
    position = lax.broadcasted_iota(jnp.int32, (pair, positions), 1)

    @pl.loop(0, steps)
    def _(step):
        for copy in cache_copies(step):
            copy.wait()

        @pl.when(step + STEPS_AHEAD < steps)
        def _():
            for copy in cache_copies(step + STEPS_AHEAD):
                copy.start()

        @pl.when(step == 0)
        def _():
            weight_copy.start()
            residual_copy.start()

        first = pl.multiple_of(step * (ROWS_STEP * head_count), ROWS_STEP * head_count)
        queries = query_scr[pl.ds(first, ROWS_STEP * head_count), :]
        parts = []
        for i in range(ROWS_STEP // 2):
            row = step * ROWS_STEP + 2 * i
            keys = key_ref[pl.ds(row, 2)].reshape(2 * positions, head_size)
            asked = queries[i * pair : (i + 1) * pair].astype(jnp.bfloat16)
            both = lax.dot_general(
                asked, keys, (((1,), (1,)), ((), ())), preferred_element_type=jnp.float32
            )
            scores = jnp.where(upper, both[:, :positions], both[:, positions:]) * score_scale
            live = jnp.where(upper, lengths_ref[row], lengths_ref[row + 1])
            parts.append(jnp.where(position < live, scores, -1e30))
        scores = jnp.concatenate(parts, axis=0)
        own_keys = own_key_scr[pl.ds(first, ROWS_STEP * head_count), :]
        own_score = jnp.sum(queries * own_keys, axis=-1, keepdims=True) * score_scale
        row_max = jnp.maximum(jnp.max(scores, axis=-1, keepdims=True), own_score)
        terms = jnp.exp(scores - row_max)
        own_term = jnp.exp(own_score - row_max)
        total = jnp.sum(terms, axis=-1, keepdims=True) + own_term
        probs = (terms / total).astype(jnp.bfloat16).astype(jnp.float32)
        own_prob = (own_term / total).astype(jnp.bfloat16).astype(jnp.float32)
        parts = []
        for i in range(ROWS_STEP // 2):
            row = step * ROWS_STEP + 2 * i
            values = value_ref[pl.ds(row, 2)].reshape(2 * positions, head_size)
            prob = probs[i * pair : (i + 1) * pair]
            spread = jnp.concatenate(
                [jnp.where(upper, prob, 0.0), jnp.where(upper, 0.0, prob)], axis=1
            ).astype(jnp.bfloat16)
            parts.append(jnp.dot(spread, values, preferred_element_type=jnp.float32))
        attended = jnp.concatenate(parts, axis=0)
        own_values = own_value_scr[pl.ds(first, ROWS_STEP * head_count), :]
        attended_scr[pl.ds(first, ROWS_STEP * head_count), :] = attended + own_prob * own_values

    for head in range(head_count):
        columns = pl.ds(head * head_size, head_size)
        rows = pl.ds(head, row_count, stride=head_count)
        heads_scr[:, columns] = attended_scr[rows, :].astype(jnp.bfloat16)
    residual_copy.wait()
    weight_copy.wait()
    for piece in range(pieces):
        columns = pl.ds(piece * chunk, chunk)
        part = jnp.dot(
            heads_scr[...], weight_ref[:, columns], preferred_element_type=jnp.float32
        )
        out_ref[piece] = part.astype(jnp.bfloat16)


def run_attend(
    residual_in, query, fresh_key, fresh_value, key_cache, value_cache, lengths, column, kv_head, out_weight, pieces,
):
    row_count, positions, head_size = key_cache.shape
    width = out_weight.shape[1]
    many = query.shape[0] * query.shape[1] // head_size
    whole = pl.BlockSpec(memory_space=pltpu.VMEM)
    scalars = pl.BlockSpec(memory_space=pltpu.SMEM)
    left = pl.BlockSpec(memory_space=pltpu.HBM)
    steps = row_count // ROWS_STEP
    return pl.pallas_call(
        attend_kernel,
        out_shape=(
            jax.ShapeDtypeStruct((pieces, row_count, width // pieces), jnp.bfloat16),
            jax.ShapeDtypeStruct((row_count, width // pieces), residual_in.dtype),
        ),
        in_specs=[scalars] * 2 + [left] * 8,
        out_specs=(whole, whole),
        scratch_shapes=[
            pltpu.SMEM(lengths.shape, jnp.int32),
            pltpu.VMEM(query.shape, jnp.bfloat16),
            pltpu.VMEM(fresh_key.shape, jnp.bfloat16),
            pltpu.VMEM(fresh_value.shape, jnp.bfloat16),
            pltpu.VMEM(key_cache.shape, jnp.bfloat16),
            pltpu.VMEM(value_cache.shape, jnp.bfloat16),
            pltpu.VMEM(out_weight.shape, jnp.bfloat16),
            pltpu.VMEM((many, head_size), jnp.float32),
            pltpu.VMEM((many, head_size), jnp.float32),
            pltpu.VMEM((many, head_size), jnp.float32),
            pltpu.VMEM((many, head_size), jnp.float32),
            pltpu.VMEM(query.shape, jnp.bfloat16),
            pltpu.SemaphoreType.DMA((4,)),
            pltpu.SemaphoreType.DMA,
            pltpu.SemaphoreType.DMA((steps,)),
            pltpu.SemaphoreType.DMA((steps,)),
            pltpu.SemaphoreType.DMA,
        ],
        compiler_params=pltpu.CompilerParams(vmem_limit_bytes=60 * 1024 * 1024),
        name="attend",
    )(kv_head, column, lengths, residual_in, query, fresh_key, fresh_value, key_cache, value_cache, out_weight)


def route_kernel(ids_ref, scores_ref, residual_ref, slot_ref, weight_ref, kept_ref):
    experts, row_count = slot_ref.shape
    topk = ids_ref.shape[0]
    scores = scores_ref[...]
    weights = scores / jnp.sum(scores, axis=0, keepdims=True)
    expert = lax.broadcasted_iota(jnp.int32, (experts, row_count), 0)
    named = jnp.zeros((experts, row_count), jnp.float32)
    weight = jnp.zeros((experts, row_count), jnp.float32)
    for k in range(topk):
        match = ids_ref[k : k + 1, :] == expert
        named = named + jnp.where(match, 1.0, 0.0)
        weight = weight + jnp.where(match, weights[k : k + 1, :], 0.0)
    earlier = lax.broadcasted_iota(jnp.int32, (row_count, row_count), 0)
    later = lax.broadcasted_iota(jnp.int32, (row_count, row_count), 1)
    before = jnp.where(earlier < later, 1.0, 0.0).astype(jnp.bfloat16)
    rank = jnp.dot(named.astype(jnp.bfloat16), before, preferred_element_type=jnp.float32)
    slot_ref[...] = jnp.where(named > 0.0, rank, -1.0).astype(jnp.int32)
    weight_ref[...] = weight
    kept_ref[...] = residual_ref[...]


def run_route(expert_ids, gate_scores, residual, experts_all):
    row_count = expert_ids.shape[0]
    whole = pl.BlockSpec(memory_space=pltpu.VMEM)
    return pl.pallas_call(
        route_kernel,
        out_shape=(
            jax.ShapeDtypeStruct((experts_all, row_count), jnp.int32),
            jax.ShapeDtypeStruct((experts_all, row_count), jnp.float32),
            jax.ShapeDtypeStruct(residual.shape, residual.dtype),
        ),
        in_specs=[whole] * 3,
        out_specs=(whole, whole, whole),
        compiler_params=pltpu.CompilerParams(vmem_limit_bytes=4 * 1024 * 1024),
        cost_estimate=pl.CostEstimate(
            flops=60_000_000_000, bytes_accessed=4_000_000, transcendentals=0
        ),
        name="route",
    )(expert_ids.T, gate_scores.T, residual)


def select_kernel(pieces_ref, residual_ref, slot_ref, hidden_ref, outgoing_ref):
    sources = pieces_ref.shape[0]
    experts, slots, chunk = outgoing_ref.shape
    row_count = slot_ref.shape[1]
    proj = pieces_ref[0].astype(jnp.float32)
    for source in range(1, sources):
        proj = proj + pieces_ref[source].astype(jnp.float32)
    hidden = (residual_ref[...].astype(jnp.float32) + proj).astype(jnp.bfloat16)
    hidden_ref[...] = hidden
    group = row_count // slots
    place = lax.broadcasted_iota(jnp.int32, (group, slots, row_count), 1)
    for first in range(0, experts, group):
        chosen = slot_ref[pl.ds(first, group), :][:, None, :] == place
        selector = jnp.where(chosen, 1.0, 0.0).reshape(group * slots, row_count)
        rows = jnp.dot(selector.astype(jnp.bfloat16), hidden, preferred_element_type=jnp.float32)
        outgoing_ref[pl.ds(first, group)] = rows.astype(jnp.bfloat16).reshape(group, slots, chunk)


def run_select(pieces, residual, slot, slots):
    experts, row_count = slot.shape
    chunk = pieces.shape[2]
    whole = pl.BlockSpec(memory_space=pltpu.VMEM)
    return pl.pallas_call(
        select_kernel,
        out_shape=(
            jax.ShapeDtypeStruct((row_count, chunk), jnp.bfloat16),
            jax.ShapeDtypeStruct((experts, slots, chunk), jnp.bfloat16),
        ),
        in_specs=[whole] * 3,
        out_specs=(whole, whole),
        compiler_params=pltpu.CompilerParams(vmem_limit_bytes=8 * 1024 * 1024),
        cost_estimate=pl.CostEstimate(flops=115_000_000_000, bytes_accessed=4_000_000, transcendentals=0),
        name="select",
    )(pieces, residual, slot)


def experts_kernel(rows_ref, gain_ref, gate_ref, up_ref, down_ref, out_ref, gained_ref, act_ref):
    replicas, pieces, slots, chunk = rows_ref.shape
    total = replicas * slots
    width = pieces * chunk
    squares = jnp.zeros((total, chunk), jnp.float32)
    for piece in range(pieces):
        part = rows_ref[:, piece].reshape(total, chunk).astype(jnp.float32)
        columns = pl.ds(piece * chunk, chunk)
        squares = squares + part * part
        gained_ref[:, columns] = (part * gain_ref[:, columns]).astype(jnp.bfloat16)
    spread = jnp.sum(squares, axis=-1, keepdims=True) * (1.0 / width)
    scale = lax.rsqrt(spread + 1e-06)
    for first in range(0, gate_ref.shape[1], chunk):
        units = pl.ds(first, chunk)
        gates = scale * jnp.dot(
            gained_ref[...], gate_ref[:, units], preferred_element_type=jnp.float32
        )
        ups = scale * jnp.dot(
            gained_ref[...], up_ref[:, units], preferred_element_type=jnp.float32
        )
        act_ref[:, units] = (gates / (1.0 + jnp.exp(-gates)) * ups).astype(jnp.bfloat16)
    for piece in range(pieces):
        columns = pl.ds(piece * chunk, chunk)
        part = jnp.dot(act_ref[...], down_ref[:, columns], preferred_element_type=jnp.float32)
        block, inner = divmod(piece * chunk, out_ref.shape[3])
        out_ref[:, block, :, pl.ds(inner, chunk)] = part.astype(jnp.bfloat16).reshape(
            replicas, slots, chunk
        )


def run_experts(rows, norm_gain, weights, blocks):
    replicas, pieces, slots, chunk = rows.shape
    width, hidden_units = weights[0].shape
    total = replicas * slots
    whole = pl.BlockSpec(memory_space=pltpu.VMEM)
    return pl.pallas_call(
        experts_kernel,
        out_shape=jax.ShapeDtypeStruct((replicas, blocks, slots, width // blocks), jnp.bfloat16),
        in_specs=[whole] * 5,
        out_specs=whole,
        scratch_shapes=[
            pltpu.VMEM((total, width), jnp.bfloat16),
            pltpu.VMEM((total, hidden_units), jnp.bfloat16),
        ],
        compiler_params=pltpu.CompilerParams(vmem_limit_bytes=16 * 1024 * 1024),
        name="experts",
    )(rows, norm_gain.reshape(1, width), *weights)


def spread_kernel(line_ref, slot_ref, weight_ref, spread_ref):
    experts, row_count = slot_ref.shape
    total = spread_ref.shape[2]
    slots = total // (experts // LINES)
    step = 256
    slot = slot_ref[...].astype(jnp.float32).T.astype(jnp.bfloat16)
    weight = weight_ref[...].T
    coarse = weight.astype(jnp.bfloat16)
    fine = (weight - coarse.astype(jnp.float32)).astype(jnp.bfloat16)
    expert = lax.broadcasted_iota(jnp.int32, (experts, step), 0)
    lane = lax.broadcasted_iota(jnp.int32, (experts, step), 1)
    row_lane = lax.broadcasted_iota(jnp.int32, (row_count, step), 1)
    for first in range(0, total, step):
        begin = lane + first - lax.rem(lane + first, slots)
        expand = jnp.where(begin * LINES == (expert - line_ref[0]) * slots, 1.0, 0.0)
        expand = expand.astype(jnp.bfloat16)
        here = jnp.dot(slot, expand, preferred_element_type=jnp.float32)
        chosen = here == lax.rem(row_lane + first, slots).astype(jnp.float32)
        for part, values in enumerate((coarse, fine)):
            spread = jnp.dot(values, expand, preferred_element_type=jnp.float32)
            spread_ref[part, :, pl.ds(first, step)] = jnp.where(chosen, spread, 0.0).astype(
                jnp.bfloat16
            )


def run_spread(line, slot, row_weight, slots):
    experts, row_count = slot.shape
    whole = pl.BlockSpec(memory_space=pltpu.VMEM)
    return pl.pallas_call(
        spread_kernel,
        out_shape=jax.ShapeDtypeStruct((2, row_count, experts // LINES * slots), jnp.bfloat16),
        in_specs=[pl.BlockSpec(memory_space=pltpu.SMEM), whole, whole],
        out_specs=whole,
        compiler_params=pltpu.CompilerParams(vmem_limit_bytes=4 * 1024 * 1024),
        name="spread",
    )(line, slot, row_weight)


def combine_kernel(line_ref, spread_ref, returned_ref, hidden_ref, out_ref, sum_ref):
    experts, slots, width = returned_ref.shape
    chunk = hidden_ref.shape[1]
    rows = returned_ref[...].reshape(experts * slots, width)
    sum_ref[...] = jnp.dot(spread_ref[0], rows, preferred_element_type=jnp.float32) + jnp.dot(
        spread_ref[1], rows, preferred_element_type=jnp.float32
    )
    own = pl.ds(pl.multiple_of(line_ref[0] * chunk, chunk), chunk)
    sum_ref[:, own] += hidden_ref[...].astype(jnp.float32)
    out_ref[...] = sum_ref[...].reshape(out_ref.shape).astype(jnp.bfloat16)


def run_combine(line, spread, returned, hidden, parts):
    row_count = hidden.shape[0]
    width = returned.shape[2]
    whole = pl.BlockSpec(memory_space=pltpu.VMEM)
    return pl.pallas_call(
        combine_kernel,
        out_shape=jax.ShapeDtypeStruct((parts, row_count // parts, width), jnp.bfloat16),
        in_specs=[pl.BlockSpec(memory_space=pltpu.SMEM), whole, whole, whole],
        out_specs=whole,
        scratch_shapes=[pltpu.VMEM((row_count, width), jnp.float32)],
        compiler_params=pltpu.CompilerParams(vmem_limit_bytes=8 * 1024 * 1024),
        name="combine",
    )(line, spread, returned, hidden)


def finish_kernel(parts_ref, out_ref):
    sources, _, width = parts_ref.shape
    for block in range(sources // LINES):
        total = parts_ref[block * LINES].astype(jnp.float32)
        for line in range(1, LINES):
            total = total + parts_ref[block * LINES + line].astype(jnp.float32)
        out_ref[:, pl.ds(block * width, width)] = total.astype(jnp.bfloat16)


def run_finish(parts):
    sources, row_count, width = parts.shape
    whole = pl.BlockSpec(memory_space=pltpu.VMEM)
    return pl.pallas_call(
        finish_kernel,
        out_shape=jax.ShapeDtypeStruct((row_count, sources // LINES * width), jnp.bfloat16),
        in_specs=[whole],
        out_specs=whole,
        compiler_params=pltpu.CompilerParams(vmem_limit_bytes=4 * 1024 * 1024),
        name="finish",
    )(parts)


def shards(
    residual_in,
    query,
    fresh_key,
    fresh_value,
    key_cache,
    value_cache,
    lengths,
    out_weight,
    norm_gain,
    expert_ids,
    gate_scores,
    w_gate,
    w_up,
    w_down,
):
    both = ("dp", *TENSOR)
    row_count, width = residual_in.shape
    tensor_width = lax.axis_size(TENSOR)
    replica_count = lax.axis_size("dp")
    experts_all = replica_count * tensor_width
    column = lax.axis_index(TENSOR)
    chunk = width // tensor_width
    cap_slots = 2 * max(1, row_count * expert_ids.shape[1] // experts_all)

    kv_head = (column // (tensor_width // fresh_key.shape[1])).astype(jnp.int32).reshape(1)
    own_column = column.astype(jnp.int32).reshape(1)
    partial, residual = run_attend(
        residual_in, query, fresh_key, fresh_value, key_cache[:, 0], value_cache[:, 0], lengths,
        own_column, kv_head, out_weight, tensor_width,
    )
    pieces = lax.all_to_all(partial, TENSOR, split_axis=0, concat_axis=0, tiled=True)
    slot, row_weight, residual = run_route(expert_ids, gate_scores, residual, experts_all)
    hidden, outgoing = run_select(pieces, residual, slot, cap_slots)
    received = lax.all_to_all(outgoing, both, split_axis=0, concat_axis=0, tiled=True)

    weights = [w_gate[0], w_up[0], w_down[0]]
    rows = received.reshape(replica_count, tensor_width, cap_slots, chunk)
    answered = run_experts(rows, norm_gain, weights, tensor_width // LINES)
    answered = answered.reshape(experts_all // LINES, cap_slots, width // (tensor_width // LINES))
    slot, row_weight, answered = lax.optimization_barrier((slot, row_weight, answered))
    returned = lax.all_to_all(
        answered, ("dp", "column"), split_axis=0, concat_axis=0, tiled=True
    )
    line = lax.axis_index("line").astype(jnp.int32).reshape(1)
    spread = run_spread(line, slot, row_weight, cap_slots)
    own = lax.all_to_all(
        run_combine(line, spread, returned, hidden, tensor_width),
        TENSOR,
        split_axis=0,
        concat_axis=0,
        tiled=True,
    )
    return run_finish(own)


def solution(mesh):
    shape = (mesh.shape["dp"], mesh.shape["tensor"] // LINES, LINES)
    mesh = Mesh(mesh.devices.reshape(shape), ("dp", *TENSOR))
    placed = (
        P("dp", None),
        P("dp", TENSOR),
        P("dp", None, None),
        P("dp", None, None),
        P("dp", TENSOR, None, None),
        P("dp", TENSOR, None, None),
        P("dp"),
        P(TENSOR, None),
        P(),
        P("dp", None),
        P("dp", None),
        P(("dp", *TENSOR), None, None),
        P(("dp", *TENSOR), None, None),
        P(("dp", *TENSOR), None, None),
    )
    return jax.shard_map(
        shards, mesh=mesh, in_specs=placed, out_specs=P(("dp", *TENSOR), None), check_vma=False
    )
```

```python
import jax
import jax.numpy as jnp
from jax import lax
from jax.experimental import pallas as pl
from jax.experimental.pallas import tpu as pltpu
from jax.sharding import Mesh
from jax.sharding import PartitionSpec as P

TENSOR = ("column", "line")
LINES = 4


ROWS_STEP = 32
STEPS_AHEAD = 3


def attend_kernel(
    head_ref, column_ref, lengths_hbm, residual_hbm, query_hbm, fresh_key_hbm, fresh_value_hbm, key_hbm, value_hbm, weight_hbm,
    out_ref, residual_ref,
    lengths_ref, query_ref, fresh_key_ref, fresh_value_ref, key_ref, value_ref, weight_ref,
    query_scr, own_key_scr, own_value_scr, attended_scr, heads_scr,
    small_sem, residual_sem, key_sem, value_sem, weight_sem,
):
    row_count, positions, head_size = key_ref.shape
    head_count = query_ref.shape[1] // head_size
    pieces, _, chunk = out_ref.shape
    steps = row_count // ROWS_STEP
    score_scale = head_size ** (-0.5)

    def cache_copies(step):
        rows = pl.ds(step * ROWS_STEP, ROWS_STEP)
        return (
            pltpu.make_async_copy(key_hbm.at[rows], key_ref.at[rows], key_sem.at[step]),
            pltpu.make_async_copy(value_hbm.at[rows], value_ref.at[rows], value_sem.at[step]),
        )

    weight_copy = pltpu.make_async_copy(weight_hbm, weight_ref, weight_sem)
    own = pl.ds(pl.multiple_of(column_ref[0] * chunk, chunk), chunk)
    residual_copy = pltpu.make_async_copy(residual_hbm.at[:, own], residual_ref, residual_sem)
    small = [
        pltpu.make_async_copy(query_hbm, query_ref, small_sem.at[0]),
        pltpu.make_async_copy(fresh_key_hbm, fresh_key_ref, small_sem.at[1]),
        pltpu.make_async_copy(fresh_value_hbm, fresh_value_ref, small_sem.at[2]),
        pltpu.make_async_copy(lengths_hbm, lengths_ref, small_sem.at[3]),
    ]
    for copy in small:
        copy.start()
    for step in range(STEPS_AHEAD):
        for copy in cache_copies(step):
            copy.start()
    for copy in small:
        copy.wait()

    group = lax.broadcasted_iota(jnp.int32, fresh_key_ref.shape, 1) == head_ref[0]
    own_key = jnp.sum(jnp.where(group, fresh_key_ref[...].astype(jnp.float32), 0.0), axis=1)
    own_value = jnp.sum(jnp.where(group, fresh_value_ref[...].astype(jnp.float32), 0.0), axis=1)
    for head in range(head_count):
        rows = pl.ds(head, row_count, stride=head_count)
        columns = pl.ds(head * head_size, head_size)
        query_scr[rows, :] = query_ref[:, columns].astype(jnp.float32)
        own_key_scr[rows, :] = own_key
        own_value_scr[rows, :] = own_value

    pair = 2 * head_count
    upper = lax.broadcasted_iota(jnp.int32, (pair, positions), 0) < head_count
    position = lax.broadcasted_iota(jnp.int32, (pair, positions), 1)

    @pl.loop(0, steps)
    def _(step):
        for copy in cache_copies(step):
            copy.wait()

        @pl.when(step + STEPS_AHEAD < steps)
        def _():
            for copy in cache_copies(step + STEPS_AHEAD):
                copy.start()

        @pl.when(step == 0)
        def _():
            weight_copy.start()
            residual_copy.start()

        first = pl.multiple_of(step * (ROWS_STEP * head_count), ROWS_STEP * head_count)
        queries = query_scr[pl.ds(first, ROWS_STEP * head_count), :]
        parts = []
        for i in range(ROWS_STEP // 2):
            row = step * ROWS_STEP + 2 * i
            keys = key_ref[pl.ds(row, 2)].reshape(2 * positions, head_size)
            asked = queries[i * pair : (i + 1) * pair].astype(jnp.bfloat16)
            both = lax.dot_general(
                asked, keys, (((1,), (1,)), ((), ())), preferred_element_type=jnp.float32
            )
            scores = jnp.where(upper, both[:, :positions], both[:, positions:]) * score_scale
            live = jnp.where(upper, lengths_ref[row], lengths_ref[row + 1])
            parts.append(jnp.where(position < live, scores, -1e30))
        scores = jnp.concatenate(parts, axis=0)
        own_keys = own_key_scr[pl.ds(first, ROWS_STEP * head_count), :]
        own_score = jnp.sum(queries * own_keys, axis=-1, keepdims=True) * score_scale
        row_max = jnp.maximum(jnp.max(scores, axis=-1, keepdims=True), own_score)
        terms = jnp.exp(scores - row_max)
        own_term = jnp.exp(own_score - row_max)
        total = jnp.sum(terms, axis=-1, keepdims=True) + own_term
        probs = (terms / total).astype(jnp.bfloat16).astype(jnp.float32)
        own_prob = (own_term / total).astype(jnp.bfloat16).astype(jnp.float32)
        parts = []
        for i in range(ROWS_STEP // 2):
            row = step * ROWS_STEP + 2 * i
            values = value_ref[pl.ds(row, 2)].reshape(2 * positions, head_size)
            prob = probs[i * pair : (i + 1) * pair]
            spread = jnp.concatenate(
                [jnp.where(upper, prob, 0.0), jnp.where(upper, 0.0, prob)], axis=1
            ).astype(jnp.bfloat16)
            parts.append(jnp.dot(spread, values, preferred_element_type=jnp.float32))
        attended = jnp.concatenate(parts, axis=0)
        own_values = own_value_scr[pl.ds(first, ROWS_STEP * head_count), :]
        attended_scr[pl.ds(first, ROWS_STEP * head_count), :] = attended + own_prob * own_values

    for head in range(head_count):
        columns = pl.ds(head * head_size, head_size)
        rows = pl.ds(head, row_count, stride=head_count)
        heads_scr[:, columns] = attended_scr[rows, :].astype(jnp.bfloat16)
    residual_copy.wait()
    weight_copy.wait()
    for piece in range(pieces):
        columns = pl.ds(piece * chunk, chunk)
        part = jnp.dot(
            heads_scr[...], weight_ref[:, columns], preferred_element_type=jnp.float32
        )
        out_ref[piece] = part.astype(jnp.bfloat16)


def run_attend(
    residual_in, query, fresh_key, fresh_value, key_cache, value_cache, lengths, column, kv_head, out_weight, pieces,
):
    row_count, positions, head_size = key_cache.shape
    width = out_weight.shape[1]
    many = query.shape[0] * query.shape[1] // head_size
    whole = pl.BlockSpec(memory_space=pltpu.VMEM)
    scalars = pl.BlockSpec(memory_space=pltpu.SMEM)
    left = pl.BlockSpec(memory_space=pltpu.HBM)
    steps = row_count // ROWS_STEP
    return pl.pallas_call(
        attend_kernel,
        out_shape=(
            jax.ShapeDtypeStruct((pieces, row_count, width // pieces), jnp.bfloat16),
            jax.ShapeDtypeStruct((row_count, width // pieces), residual_in.dtype),
        ),
        in_specs=[scalars] * 2 + [left] * 8,
        out_specs=(whole, whole),
        scratch_shapes=[
            pltpu.SMEM(lengths.shape, jnp.int32),
            pltpu.VMEM(query.shape, jnp.bfloat16),
            pltpu.VMEM(fresh_key.shape, jnp.bfloat16),
            pltpu.VMEM(fresh_value.shape, jnp.bfloat16),
            pltpu.VMEM(key_cache.shape, jnp.bfloat16),
            pltpu.VMEM(value_cache.shape, jnp.bfloat16),
            pltpu.VMEM(out_weight.shape, jnp.bfloat16),
            pltpu.VMEM((many, head_size), jnp.float32),
            pltpu.VMEM((many, head_size), jnp.float32),
            pltpu.VMEM((many, head_size), jnp.float32),
            pltpu.VMEM((many, head_size), jnp.float32),
            pltpu.VMEM(query.shape, jnp.bfloat16),
            pltpu.SemaphoreType.DMA((4,)),
            pltpu.SemaphoreType.DMA,
            pltpu.SemaphoreType.DMA((steps,)),
            pltpu.SemaphoreType.DMA((steps,)),
            pltpu.SemaphoreType.DMA,
        ],
        compiler_params=pltpu.CompilerParams(vmem_limit_bytes=60 * 1024 * 1024),
        name="attend",
    )(kv_head, column, lengths, residual_in, query, fresh_key, fresh_value, key_cache, value_cache, out_weight)


def route_kernel(ids_ref, scores_ref, residual_ref, slot_ref, weight_ref, kept_ref):
    experts, row_count = slot_ref.shape
    topk = ids_ref.shape[0]
    scores = scores_ref[...]
    weights = scores / jnp.sum(scores, axis=0, keepdims=True)
    expert = lax.broadcasted_iota(jnp.int32, (experts, row_count), 0)
    named = jnp.zeros((experts, row_count), jnp.float32)
    weight = jnp.zeros((experts, row_count), jnp.float32)
    for k in range(topk):
        match = ids_ref[k : k + 1, :] == expert
        named = named + jnp.where(match, 1.0, 0.0)
        weight = weight + jnp.where(match, weights[k : k + 1, :], 0.0)
    earlier = lax.broadcasted_iota(jnp.int32, (row_count, row_count), 0)
    later = lax.broadcasted_iota(jnp.int32, (row_count, row_count), 1)
    before = jnp.where(earlier < later, 1.0, 0.0).astype(jnp.bfloat16)
    rank = jnp.dot(named.astype(jnp.bfloat16), before, preferred_element_type=jnp.float32)
    slot_ref[...] = jnp.where(named > 0.0, rank, -1.0).astype(jnp.int32)
    weight_ref[...] = weight
    kept_ref[...] = residual_ref[...]


def run_route(expert_ids, gate_scores, residual, experts_all):
    row_count = expert_ids.shape[0]
    whole = pl.BlockSpec(memory_space=pltpu.VMEM)
    return pl.pallas_call(
        route_kernel,
        out_shape=(
            jax.ShapeDtypeStruct((experts_all, row_count), jnp.int32),
            jax.ShapeDtypeStruct((experts_all, row_count), jnp.float32),
            jax.ShapeDtypeStruct(residual.shape, residual.dtype),
        ),
        in_specs=[whole] * 3,
        out_specs=(whole, whole, whole),
        compiler_params=pltpu.CompilerParams(vmem_limit_bytes=4 * 1024 * 1024),
        cost_estimate=pl.CostEstimate(
            flops=60_000_000_000, bytes_accessed=4_000_000, transcendentals=0
        ),
        name="route",
    )(expert_ids.T, gate_scores.T, residual)


def select_kernel(pieces_ref, residual_ref, slot_ref, hidden_ref, outgoing_ref):
    sources = pieces_ref.shape[0]
    experts, slots, chunk = outgoing_ref.shape
    row_count = slot_ref.shape[1]
    proj = pieces_ref[0].astype(jnp.float32)
    for source in range(1, sources):
        proj = proj + pieces_ref[source].astype(jnp.float32)
    hidden = (residual_ref[...].astype(jnp.float32) + proj).astype(jnp.bfloat16)
    hidden_ref[...] = hidden
    group = row_count // slots
    place = lax.broadcasted_iota(jnp.int32, (group, slots, row_count), 1)
    for first in range(0, experts, group):
        chosen = slot_ref[pl.ds(first, group), :][:, None, :] == place
        selector = jnp.where(chosen, 1.0, 0.0).reshape(group * slots, row_count)
        rows = jnp.dot(selector.astype(jnp.bfloat16), hidden, preferred_element_type=jnp.float32)
        outgoing_ref[pl.ds(first, group)] = rows.astype(jnp.bfloat16).reshape(group, slots, chunk)


def run_select(pieces, residual, slot, slots):
    experts, row_count = slot.shape
    chunk = pieces.shape[2]
    whole = pl.BlockSpec(memory_space=pltpu.VMEM)
    return pl.pallas_call(
        select_kernel,
        out_shape=(
            jax.ShapeDtypeStruct((row_count, chunk), jnp.bfloat16),
            jax.ShapeDtypeStruct((experts, slots, chunk), jnp.bfloat16),
        ),
        in_specs=[whole] * 3,
        out_specs=(whole, whole),
        compiler_params=pltpu.CompilerParams(vmem_limit_bytes=8 * 1024 * 1024),
        cost_estimate=pl.CostEstimate(flops=115_000_000_000, bytes_accessed=4_000_000, transcendentals=0),
        name="select",
    )(pieces, residual, slot)


def experts_kernel(
    rows_ref, gain_ref, gate_ref, up_ref, down_ref, out_hbm, gained_ref, act_ref, out_ref, out_sem
):
    replicas, pieces, slots, chunk = rows_ref.shape
    total = replicas * slots
    width = pieces * chunk

    def out_copy(block):
        return pltpu.make_async_copy(out_ref.at[:, block], out_hbm.at[:, block], out_sem.at[block])

    squares = jnp.zeros((total, chunk), jnp.float32)
    for piece in range(pieces):
        part = rows_ref[:, piece].reshape(total, chunk).astype(jnp.float32)
        columns = pl.ds(piece * chunk, chunk)
        squares = squares + part * part
        gained_ref[:, columns] = (part * gain_ref[:, columns]).astype(jnp.bfloat16)
    spread = jnp.sum(squares, axis=-1, keepdims=True) * (1.0 / width)
    scale = lax.rsqrt(spread + 1e-06)
    for first in range(0, gate_ref.shape[1], chunk):
        units = pl.ds(first, chunk)
        gates = scale * jnp.dot(
            gained_ref[...], gate_ref[:, units], preferred_element_type=jnp.float32
        )
        ups = scale * jnp.dot(
            gained_ref[...], up_ref[:, units], preferred_element_type=jnp.float32
        )
        act_ref[:, units] = (gates / (1.0 + jnp.exp(-gates)) * ups).astype(jnp.bfloat16)
    for piece in range(pieces):
        columns = pl.ds(piece * chunk, chunk)
        part = jnp.dot(act_ref[...], down_ref[:, columns], preferred_element_type=jnp.float32)
        block, inner = divmod(piece * chunk, out_ref.shape[3])
        out_ref[:, block, :, pl.ds(inner, chunk)] = part.astype(jnp.bfloat16).reshape(
            replicas, slots, chunk
        )
        if inner + chunk == out_ref.shape[3]:
            out_copy(block).start()
    for block in range(out_ref.shape[1]):
        out_copy(block).wait()


def run_experts(rows, norm_gain, weights, blocks):
    replicas, pieces, slots, chunk = rows.shape
    width, hidden_units = weights[0].shape
    total = replicas * slots
    whole = pl.BlockSpec(memory_space=pltpu.VMEM)
    return pl.pallas_call(
        experts_kernel,
        out_shape=jax.ShapeDtypeStruct((replicas, blocks, slots, width // blocks), jnp.bfloat16),
        in_specs=[whole] * 5,
        out_specs=pl.BlockSpec(memory_space=pltpu.HBM),
        scratch_shapes=[
            pltpu.VMEM((total, width), jnp.bfloat16),
            pltpu.VMEM((total, hidden_units), jnp.bfloat16),
            pltpu.VMEM((replicas, blocks, slots, width // blocks), jnp.bfloat16),
            pltpu.SemaphoreType.DMA((blocks,)),
        ],
        compiler_params=pltpu.CompilerParams(vmem_limit_bytes=16 * 1024 * 1024),
        name="experts",
    )(rows, norm_gain.reshape(1, width), *weights)


def spread_kernel(line_ref, slot_ref, weight_ref, spread_ref):
    experts, row_count = slot_ref.shape
    total = spread_ref.shape[2]
    slots = total // (experts // LINES)
    step = 256
    slot = slot_ref[...].astype(jnp.float32).T.astype(jnp.bfloat16)
    weight = weight_ref[...].T
    coarse = weight.astype(jnp.bfloat16)
    fine = (weight - coarse.astype(jnp.float32)).astype(jnp.bfloat16)
    expert = lax.broadcasted_iota(jnp.int32, (experts, step), 0)
    lane = lax.broadcasted_iota(jnp.int32, (experts, step), 1)
    row_lane = lax.broadcasted_iota(jnp.int32, (row_count, step), 1)
    for first in range(0, total, step):
        begin = lane + first - lax.rem(lane + first, slots)
        expand = jnp.where(begin * LINES == (expert - line_ref[0]) * slots, 1.0, 0.0)
        expand = expand.astype(jnp.bfloat16)
        here = jnp.dot(slot, expand, preferred_element_type=jnp.float32)
        chosen = here == lax.rem(row_lane + first, slots).astype(jnp.float32)
        for part, values in enumerate((coarse, fine)):
            spread = jnp.dot(values, expand, preferred_element_type=jnp.float32)
            spread_ref[part, :, pl.ds(first, step)] = jnp.where(chosen, spread, 0.0).astype(
                jnp.bfloat16
            )


def run_spread(line, slot, row_weight, slots):
    experts, row_count = slot.shape
    whole = pl.BlockSpec(memory_space=pltpu.VMEM)
    return pl.pallas_call(
        spread_kernel,
        out_shape=jax.ShapeDtypeStruct((2, row_count, experts // LINES * slots), jnp.bfloat16),
        in_specs=[pl.BlockSpec(memory_space=pltpu.SMEM), whole, whole],
        out_specs=whole,
        compiler_params=pltpu.CompilerParams(vmem_limit_bytes=4 * 1024 * 1024),
        name="spread",
    )(line, slot, row_weight)


def combine_kernel(line_ref, spread_ref, returned_ref, hidden_ref, out_ref, sum_ref):
    experts, slots, width = returned_ref.shape
    chunk = hidden_ref.shape[1]
    rows = returned_ref[...].reshape(experts * slots, width)
    sum_ref[...] = jnp.dot(spread_ref[0], rows, preferred_element_type=jnp.float32) + jnp.dot(
        spread_ref[1], rows, preferred_element_type=jnp.float32
    )
    own = pl.ds(pl.multiple_of(line_ref[0] * chunk, chunk), chunk)
    sum_ref[:, own] += hidden_ref[...].astype(jnp.float32)
    out_ref[...] = sum_ref[...].reshape(out_ref.shape).astype(jnp.bfloat16)


def run_combine(line, spread, returned, hidden, parts):
    row_count = hidden.shape[0]
    width = returned.shape[2]
    whole = pl.BlockSpec(memory_space=pltpu.VMEM)
    return pl.pallas_call(
        combine_kernel,
        out_shape=jax.ShapeDtypeStruct((parts, row_count // parts, width), jnp.bfloat16),
        in_specs=[pl.BlockSpec(memory_space=pltpu.SMEM), whole, whole, whole],
        out_specs=whole,
        scratch_shapes=[pltpu.VMEM((row_count, width), jnp.float32)],
        compiler_params=pltpu.CompilerParams(vmem_limit_bytes=8 * 1024 * 1024),
        name="combine",
    )(line, spread, returned, hidden)


def finish_kernel(parts_ref, out_ref):
    sources, _, width = parts_ref.shape
    for block in range(sources // LINES):
        total = parts_ref[block * LINES].astype(jnp.float32)
        for line in range(1, LINES):
            total = total + parts_ref[block * LINES + line].astype(jnp.float32)
        out_ref[:, pl.ds(block * width, width)] = total.astype(jnp.bfloat16)


def run_finish(parts):
    sources, row_count, width = parts.shape
    whole = pl.BlockSpec(memory_space=pltpu.VMEM)
    return pl.pallas_call(
        finish_kernel,
        out_shape=jax.ShapeDtypeStruct((row_count, sources // LINES * width), jnp.bfloat16),
        in_specs=[whole],
        out_specs=whole,
        compiler_params=pltpu.CompilerParams(vmem_limit_bytes=4 * 1024 * 1024),
        name="finish",
    )(parts)


def shards(
    residual_in,
    query,
    fresh_key,
    fresh_value,
    key_cache,
    value_cache,
    lengths,
    out_weight,
    norm_gain,
    expert_ids,
    gate_scores,
    w_gate,
    w_up,
    w_down,
):
    both = ("dp", *TENSOR)
    row_count, width = residual_in.shape
    tensor_width = lax.axis_size(TENSOR)
    replica_count = lax.axis_size("dp")
    experts_all = replica_count * tensor_width
    column = lax.axis_index(TENSOR)
    chunk = width // tensor_width
    cap_slots = 2 * max(1, row_count * expert_ids.shape[1] // experts_all)

    kv_head = (column // (tensor_width // fresh_key.shape[1])).astype(jnp.int32).reshape(1)
    own_column = column.astype(jnp.int32).reshape(1)
    partial, residual = run_attend(
        residual_in, query, fresh_key, fresh_value, key_cache[:, 0], value_cache[:, 0], lengths,
        own_column, kv_head, out_weight, tensor_width,
    )
    pieces = lax.all_to_all(partial, TENSOR, split_axis=0, concat_axis=0, tiled=True)
    slot, row_weight, residual = run_route(expert_ids, gate_scores, residual, experts_all)
    hidden, outgoing = run_select(pieces, residual, slot, cap_slots)
    received = lax.all_to_all(outgoing, both, split_axis=0, concat_axis=0, tiled=True)

    weights = [w_gate[0], w_up[0], w_down[0]]
    rows = received.reshape(replica_count, tensor_width, cap_slots, chunk)
    answered = run_experts(rows, norm_gain, weights, tensor_width // LINES)
    answered = answered.reshape(experts_all // LINES, cap_slots, width // (tensor_width // LINES))
    slot, row_weight, answered = lax.optimization_barrier((slot, row_weight, answered))
    returned = lax.all_to_all(
        answered, ("dp", "column"), split_axis=0, concat_axis=0, tiled=True
    )
    line = lax.axis_index("line").astype(jnp.int32).reshape(1)
    spread = run_spread(line, slot, row_weight, cap_slots)
    own = lax.all_to_all(
        run_combine(line, spread, returned, hidden, tensor_width),
        TENSOR,
        split_axis=0,
        concat_axis=0,
        tiled=True,
    )
    return run_finish(own)


def solution(mesh):
    shape = (mesh.shape["dp"], mesh.shape["tensor"] // LINES, LINES)
    mesh = Mesh(mesh.devices.reshape(shape), ("dp", *TENSOR))
    placed = (
        P("dp", None),
        P("dp", TENSOR),
        P("dp", None, None),
        P("dp", None, None),
        P("dp", TENSOR, None, None),
        P("dp", TENSOR, None, None),
        P("dp"),
        P(TENSOR, None),
        P(),
        P("dp", None),
        P("dp", None),
        P(("dp", *TENSOR), None, None),
        P(("dp", *TENSOR), None, None),
        P(("dp", *TENSOR), None, None),
    )
    return jax.shard_map(
        shards, mesh=mesh, in_specs=placed, out_specs=P(("dp", *TENSOR), None), check_vma=False
    )
```
